128 devices in a mesh: section: 16 (over z_hi, y, core), seq: 8 (over x, z_lo).
Axes of the slice: x: 4, y: 4, z: 4 (z_hi: 2, z_lo: 2; z = z_hi * 2 + z_lo), core: 2. Of those that a mesh axis runs over, the one named last changes fastest.
Arguments:
- stash_query: bfloat16 [16, 1, 1536, 8192], P('section', None, 'seq'), may hold values from -8 to 8
- stash_key: bfloat16 [16, 1, 1536, 1024], P('section', None, 'seq'), may hold values from -8 to 8
- stashed_value_inputs: bfloat16 [16, 1, 1536, 1024], P('section', None, 'seq'), may hold values from -6 to 6
- grad_out: bfloat16 [16, 1, 1536, 8192], P('section', None, 'seq'), may hold values from -6 to 6
- partner: int32 [16], replicated, may hold values from 0 to 15, as said below
- span_order: int32 [16], replicated, may hold values from 0 to 15, each once
Outputs:
- grad_query: bfloat16 [16, 1, 1536, 8192], P('section', None, 'seq')
- grad_key: bfloat16 [16, 1, 1536, 1024], P('section', None, 'seq')
- grad_value: bfloat16 [16, 1, 1536, 1024], P('section', None, 'seq')
The draws below stay inside these ranges and needn't reach their ends.
Inputs may be any that keep to these rules, and one draw needn't show every extreme that they name: partner[s] = s XOR p for one p of 1 to 15, the same p for every s.
All inputs are finite; a program needn't handle non-finite values.
Results may differ from the reference program's by a relative error of at most 0.0045.
The reference program's roundings to bfloat16 on the way count: a program that leaves them out, or rounds other values in their place, can miss the bound.
Values may be sent and summed in bfloat16 or wider, within the bound.
A program may use at most 192 MiB of HBM per device.

```python
import jax
import jax.numpy as jnp
from jax import lax

QUERY_HEADS = 64
KEY_VALUE_HEADS = 8
HEAD_SIZE = 128
SECTION_LAYERS = 1
RELAY_SECTIONS = 16
SEQUENCE_TOKENS = 1536
SPANS = 16
SPAN = 96


def draw_stash_query(key, part):
    output_values = jax.random.truncated_normal(jax.random.fold_in(key, 11), -6.0, 6.0, (RELAY_SECTIONS, SECTION_LAYERS, SEQUENCE_TOKENS, QUERY_HEADS, HEAD_SIZE), jnp.float32)
    return output_values.reshape(RELAY_SECTIONS, SECTION_LAYERS, SEQUENCE_TOKENS, QUERY_HEADS * HEAD_SIZE).astype(jnp.bfloat16)


def draw_stash_key(key, part):
    output_values = jax.random.truncated_normal(jax.random.fold_in(key, 12), -6.0, 6.0, (RELAY_SECTIONS, SECTION_LAYERS, SEQUENCE_TOKENS, KEY_VALUE_HEADS, HEAD_SIZE), jnp.float32)
    return output_values.reshape(RELAY_SECTIONS, SECTION_LAYERS, SEQUENCE_TOKENS, KEY_VALUE_HEADS * HEAD_SIZE).astype(jnp.bfloat16)


def draw_partner(key, part):
    wide_draw = jax.random.randint(jax.random.fold_in(key, 7919), (), 0, 1073741823, dtype=jnp.int32)
    pair_bits = 1 + wide_draw % (RELAY_SECTIONS - 1)
    return jnp.bitwise_xor(jnp.arange(RELAY_SECTIONS, dtype=jnp.int32), pair_bits).astype(jnp.int32)


def steps_of(stream_key, extent, split, smallest, largest):
    gain = 1.0
    for position, blocks in split:
        draws = jax.random.uniform(jax.random.fold_in(jax.random.fold_in(stream_key, 6), position), (blocks,), jnp.float32, smallest / len(split), largest / len(split))
        gain = gain * jnp.repeat(jnp.exp(draws), extent[position] // blocks).reshape((-1,) + (1,) * (len(extent) - 1 - position))
    return gain


def centred(own_key, extent, deviation, most, split=(), kind=jnp.bfloat16):
    gain = steps_of(own_key, extent, split, -0.22, 0.18) if split else 1.0
    entries = jax.random.normal(own_key, extent, jnp.float32) * deviation * gain
    return jnp.minimum(jnp.maximum(entries, -most), most).astype(kind)


def setup_inputs(seed: int = 0) -> dict:
    keys = jax.random.split(jax.random.key(seed), 7)
    stash_query = draw_stash_query(jax.random.fold_in(keys[6], 71), 0)
    stash_key = draw_stash_key(jax.random.fold_in(keys[6], 71), 0)
    stashed_value_inputs = centred(keys[2], (RELAY_SECTIONS, SECTION_LAYERS, SEQUENCE_TOKENS, KEY_VALUE_HEADS * HEAD_SIZE), 1.0, 6.0, ((0, 16), (2, 8)))
    grad_out = centred(keys[3], (RELAY_SECTIONS, SECTION_LAYERS, SEQUENCE_TOKENS, QUERY_HEADS * HEAD_SIZE), 1.0, 6.0, ((0, 16), (2, 8)))
    partner = draw_partner(jax.random.fold_in(keys[6], 71), 0)
    span_order = jax.random.permutation(keys[5], SPANS).astype(jnp.int32)
    return {"stash_query": stash_query, "stash_key": stash_key, "stashed_value_inputs": stashed_value_inputs, "grad_out": grad_out, "partner": partner, "span_order": span_order}


def frequencies(head_width):
    return jnp.power(jnp.float32(1000000.0), -jnp.arange(0, head_width, 2).astype(jnp.float32) / head_width)


def apply_rotary_heads(vectors, token_index_list, orientation):
    half_width = vectors.shape[-1] // 2
    angles = token_index_list.astype(jnp.float32)[:, None] * frequencies(vectors.shape[-1])[None, :]
    cosine_table = jnp.cos(angles)[:, None, :]
    sine_table = jnp.sin(angles)[:, None, :]
    first_half = vectors[..., :half_width]
    second_half = vectors[..., half_width:]
    return jnp.concatenate([first_half * cosine_table - orientation * second_half * sine_table,
                            second_half * cosine_table + orientation * first_half * sine_table], axis=-1)


def attend_group(rotated_queries, rotated_keys, value_row_block, gradient_rows, query_pos, key_pos):
    score_scale = rotated_queries.shape[-1] ** -0.5
    query_wide = rotated_queries.astype(jnp.float32)
    key_wide = rotated_keys.astype(jnp.float32)
    value_wide = value_row_block.astype(jnp.float32)
    grad_wide = gradient_rows.astype(jnp.float32)
    scores = jnp.einsum("qrd,kd->rqk", query_wide, key_wide) * score_scale
    scores = jnp.where(key_pos[None, None, :] <= query_pos[None, :, None], scores, -jnp.inf)
    shifted = jnp.exp(scores - jnp.max(scores, axis=-1, keepdims=True))
    attention_weights = shifted / jnp.sum(shifted, axis=-1, keepdims=True)
    weights_low = lax.optimization_barrier(attention_weights.astype(jnp.bfloat16)).astype(jnp.float32)
    grad_weights = jnp.einsum("qrd,kd->rqk", grad_wide, value_wide)
    row_delta = jnp.sum(attention_weights * grad_weights, axis=-1, keepdims=True)
    grad_scores = lax.optimization_barrier((attention_weights * (grad_weights - row_delta)).astype(jnp.bfloat16)).astype(jnp.float32)
    grad_query_rot = jnp.einsum("rqk,kd->qrd", grad_scores, key_wide) * score_scale
    rotated_key_gradient = jnp.einsum("rqk,qrd->kd", grad_scores, query_wide) * score_scale
    summed_value_gradient = jnp.einsum("rqk,qrd->kd", weights_low, grad_wide)
    return grad_query_rot, rotated_key_gradient, summed_value_gradient


def reference(stash_query, stash_key, stashed_value_inputs, grad_out, partner, span_order):
    row_index = jnp.arange(SEQUENCE_TOKENS, dtype=jnp.int32)
    token_index_list = span_order[row_index // SPAN] * SPAN + row_index % SPAN
    queries_per_group = QUERY_HEADS // KEY_VALUE_HEADS

    def one_layer(query, key_row_block, value_row_block, gradient_rows):
        rotated_queries = apply_rotary_heads(query.reshape(SEQUENCE_TOKENS, QUERY_HEADS, HEAD_SIZE).astype(jnp.float32), token_index_list, 1.0).astype(jnp.bfloat16)
        rotated_keys = apply_rotary_heads(key_row_block.reshape(SEQUENCE_TOKENS, KEY_VALUE_HEADS, HEAD_SIZE).astype(jnp.float32), token_index_list, 1.0).astype(jnp.bfloat16)
        rotated_queries = lax.optimization_barrier(rotated_queries)
        rotated_keys = lax.optimization_barrier(rotated_keys)
        grouped_heads = (rotated_queries.reshape(SEQUENCE_TOKENS, KEY_VALUE_HEADS, queries_per_group, HEAD_SIZE).transpose(1, 0, 2, 3),
                   rotated_keys.transpose(1, 0, 2),
                   value_row_block.reshape(SEQUENCE_TOKENS, KEY_VALUE_HEADS, HEAD_SIZE).transpose(1, 0, 2),
                   gradient_rows.reshape(SEQUENCE_TOKENS, KEY_VALUE_HEADS, queries_per_group, HEAD_SIZE).transpose(1, 0, 2, 3))
        grad_query_rot, rotated_key_gradient, summed_value_gradient = lax.map(
            lambda pieces: attend_group(pieces[0], pieces[1], pieces[2], pieces[3], token_index_list, token_index_list), grouped_heads)
        grad_query_rot = grad_query_rot.transpose(1, 0, 2, 3).reshape(SEQUENCE_TOKENS, QUERY_HEADS, HEAD_SIZE)
        rotated_key_gradient = rotated_key_gradient.transpose(1, 0, 2)
        query_result = apply_rotary_heads(grad_query_rot, token_index_list, -1.0).astype(jnp.bfloat16).reshape(SEQUENCE_TOKENS, QUERY_HEADS * HEAD_SIZE)
        key_gradient_output = apply_rotary_heads(rotated_key_gradient, token_index_list, -1.0).astype(jnp.bfloat16).reshape(SEQUENCE_TOKENS, KEY_VALUE_HEADS * HEAD_SIZE)
        value_gradient_output = summed_value_gradient.transpose(1, 0, 2).astype(jnp.bfloat16).reshape(SEQUENCE_TOKENS, KEY_VALUE_HEADS * HEAD_SIZE)
        return query_result, key_gradient_output, value_gradient_output

    def one_section(section_index):
        source = partner[section_index]
        query_all = lax.dynamic_index_in_dim(stash_query, source, 0, keepdims=False)
        key_all = lax.dynamic_index_in_dim(stash_key, source, 0, keepdims=False)
        value_all = lax.dynamic_index_in_dim(stashed_value_inputs, source, 0, keepdims=False)
        grads_all = lax.dynamic_index_in_dim(grad_out, section_index, 0, keepdims=False)
        layer_results = [one_layer(query_all[layer_index], key_all[layer_index], value_all[layer_index], grads_all[layer_index])
                         for layer_index in range(SECTION_LAYERS)]
        return tuple(jnp.stack([layer_result[slot_index] for layer_result in layer_results]) for slot_index in range(3))

    results = lax.map(one_section, jnp.arange(RELAY_SECTIONS, dtype=jnp.int32))
    return results[0], results[1], results[2]
```

```python
import functools
import math

import jax
import jax.numpy as jnp
import numpy as np
from jax import lax
from jax.experimental import pallas as pl
from jax.experimental.pallas import tpu as pltpu
from jax.sharding import PartitionSpec as P

QUERY_HEADS = 64
KEY_VALUE_HEADS = 8
HEAD_SIZE = 128
GROUP = QUERY_HEADS // KEY_VALUE_HEADS
BLOCK = 256
MESH = pl.DeviceIdType.MESH


def rotary_table(tokens):
    half = HEAD_SIZE // 2
    steps = np.arange(0, HEAD_SIZE, 2).astype(np.float32) / np.float32(HEAD_SIZE)
    frequency = np.power(np.float32(1000000.0), -steps).astype(np.float32)
    angles = np.arange(tokens, dtype=np.float32)[:, None] * frequency[None, :]
    angles = angles.astype(np.float64)
    table = np.concatenate([np.cos(angles), np.sin(angles)], axis=1).astype(np.float32)
    assert table.shape == (tokens, 2 * half)
    return table


def xor_static(index, mask):
    result = index
    bit = 1
    while bit <= mask:
        if mask & bit:
            low = lax.rem(lax.div(index, bit), 2)
            result = result + (1 - 2 * low) * bit
        bit *= 2
    return result


def wait_bytes(like, sem):
    pltpu.make_async_copy(like, like, sem).wait()


def gather_kernel(pair, seq, q_ref, k_ref, v_ref, g_ref, q_all, k_all, v_all, g_all, send, recv, own):
    section = lax.axis_index("section")
    me = lax.axis_index("seq")
    other = xor_static(section, pair)
    rows = q_ref.shape[0]
    barrier = pltpu.get_barrier_semaphore()
    for j in range(seq):
        to = lax.rem(me + j, seq)
        pl.semaphore_signal(
            barrier, inc=1, device_id={"section": other, "seq": to}, device_id_type=MESH
        )
        if j:
            pl.semaphore_signal(
                barrier, inc=1, device_id={"section": section, "seq": to}, device_id_type=MESH
            )
    pl.semaphore_wait(barrier, 2 * seq - 1)
    wide = q_ref.shape[1] // seq
    thin = k_ref.shape[1] // seq
    mine = pl.ds(pl.multiple_of(me * rows, rows), rows)

    def columns(to, width):
        return pl.ds(pl.multiple_of(to * width, width), width)

    def send_to(source, to, width, target, index, device):
        pltpu.make_async_remote_copy(
            src_ref=source.at[:, columns(to, width)],
            dst_ref=target.at[mine],
            send_sem=send.at[index],
            recv_sem=recv.at[index],
            device_id={"section": device, "seq": to},
            device_id_type=MESH,
        ).start()

    def step(j, carry):
        to = lax.rem(me + j, seq)
        send_to(k_ref, to, thin, k_all, 0, other)
        send_to(v_ref, to, thin, v_all, 1, other)
        return carry

    lax.fori_loop(0, seq, step, 0)

    def wide_step(j, carry):
        to = lax.rem(me + j, seq)
        send_to(q_ref, to, wide, q_all, 2, other)

        @pl.when(j > 0)
        def _():
            send_to(g_ref, to, wide, g_all, 3, section)

        return carry

    lax.fori_loop(0, seq, wide_step, 0)
    local = pltpu.make_async_copy(g_ref.at[:, columns(me, wide)], g_all.at[mine], own)
    local.start()
    local.wait()
    shared = pl.ds(0, rows * (seq - 1))
    for sem in (send, recv):
        wait_bytes(k_all, sem.at[0])
        wait_bytes(v_all, sem.at[1])
        wait_bytes(q_all, sem.at[2])
        wait_bytes(g_all.at[shared], sem.at[3])


def gather(pair, seq, q, k, v, g):
    rows = q.shape[0]
    any_spec = pl.BlockSpec(memory_space=pl.ANY)

    def full(a):
        return jax.ShapeDtypeStruct((rows * seq, a.shape[1] // seq), a.dtype)

    return pl.pallas_call(
        functools.partial(gather_kernel, pair, seq),
        out_shape=(full(q), full(k), full(v), full(g)),
        in_specs=[any_spec] * 4,
        out_specs=(any_spec,) * 4,
        scratch_shapes=[
            pltpu.SemaphoreType.DMA((4,)),
            pltpu.SemaphoreType.DMA((4,)),
            pltpu.SemaphoreType.DMA(()),
        ],
        compiler_params=pltpu.CompilerParams(collective_id=pair, has_side_effects=True),
        name=f"gather_{pair}",
    )(q, k, v, g)


def dot(a, b, dims):
    return lax.dot_general(a, b, (dims, ((), ())), preferred_element_type=jnp.float32)


def attend_kernel(
    seq,
    span,
    order,
    inverse,
    q_all,
    k_all,
    v_all,
    g_all,
    table,
    dq_out,
    dk_out,
    dv_out,
    cosine,
    sine,
    qs,
    ks,
    vs,
    gs,
    kt,
    dk,
    dv,
    scores,
    gains,
    dqs,
    dvs,
    parcels,
    parcel_k,
    parcel_v,
    send,
    recv,
    own,
):
    section = lax.axis_index("section")
    me = lax.axis_index("seq")
    spans = k_all.shape[0]
    tokens = spans * span
    rows = tokens // seq
    half = HEAD_SIZE // 2
    blocks = tokens // BLOCK
    scale = HEAD_SIZE**-0.5
    scale2 = scale * math.log2(math.e)
    barrier = pltpu.get_barrier_semaphore()
    for j in range(1, seq):
        pl.semaphore_signal(
            barrier,
            inc=1,
            device_id={"section": section, "seq": lax.rem(me + j, seq)},
            device_id_type=MESH,
        )
    pl.semaphore_wait(barrier, seq - 1)

    def turn(x, at, sign):
        return x * cosine[at] + sign * (pltpu.roll(x, half, 1) * sine[at])

    first = lax.broadcasted_iota(jnp.int32, (span, HEAD_SIZE), 1) < half
    for b in range(spans):
        at = pl.ds(b * span, span)
        both = table[at]
        swapped = pltpu.roll(both, half, 1)
        cosine[at] = jnp.where(first, both, swapped)
        sine[at] = jnp.where(first, -swapped, both)
        key = turn(k_all[inverse[b]].astype(jnp.float32), at, 1.0)
        ks[at] = key.astype(jnp.bfloat16)
        vs[at] = v_all[inverse[b]]
    kt[...] = ks[...].T
    dk[...] = jnp.zeros_like(dk)
    dv[...] = jnp.zeros_like(dv)
    diagonal = lax.broadcasted_iota(jnp.int32, (BLOCK, BLOCK), 0) <= lax.broadcasted_iota(
        jnp.int32, (BLOCK, BLOCK), 1
    )
    parts = BLOCK // 8

    def send_to(source, target, index, j):
        to = lax.rem(me + j, seq)
        pltpu.make_async_remote_copy(
            src_ref=source.at[pl.ds(pl.multiple_of(to * rows, rows), rows)],
            dst_ref=target,
            send_sem=send.at[index],
            recv_sem=recv.at[index],
            device_id={"section": section, "seq": to},
            device_id_type=MESH,
        ).start()

    def scatter(source, target, index):
        for j in range(1, seq):
            send_to(source, target, index, j)
        pltpu.make_async_copy(
            source.at[pl.ds(pl.multiple_of(me * rows, rows), rows)], target, own.at[index]
        ).start()

    def keep_rows(target, start, value):
        stop = start + value.shape[0]
        row = start
        while row < stop:
            b, low = row // span, row % span
            size = min(span - low, stop - row)
            target[b, pl.ds(low, size)] = value[row - start : row - start + size]
            row += size

    def head(h, carry):
        lanes = pl.ds(pl.multiple_of(h * HEAD_SIZE, HEAD_SIZE), HEAD_SIZE)
        for b in range(spans):
            at = pl.ds(b * span, span)
            query = turn(q_all[inverse[b], :, lanes].astype(jnp.float32), at, 1.0)
            qs[at] = query.astype(jnp.bfloat16)
            gs[at] = g_all[inverse[b], :, lanes]
        for i in range(blocks):
            at = pl.ds(i * BLOCK, BLOCK)
            qb = qs[at]
            gb = gs[at]
            top = None
            for c in range(i + 1):
                keys = pl.ds(c * BLOCK, BLOCK)
                s = dot(ks[keys], qb, ((1,), (1,)))
                if c == i:
                    s = jnp.where(diagonal, s, -jnp.inf)
                scores[keys] = s
                part = jnp.max(s.reshape(parts, 8, BLOCK), axis=0)
                top = part if top is None else jnp.maximum(top, part)
            top = jnp.max(top, axis=0, keepdims=True)
            total = jnp.zeros((8, BLOCK), jnp.float32)
            mixed = jnp.zeros((8, BLOCK), jnp.float32)
            for c in range(i + 1):
                keys = pl.ds(c * BLOCK, BLOCK)
                e = jnp.exp2((scores[keys] - top) * scale2)
                gain = dot(vs[keys], gb, ((1,), (1,)))
                scores[keys] = e
                gains[keys] = gain
                total = total + jnp.sum(e.reshape(parts, 8, BLOCK), axis=0)
                mixed = mixed + jnp.sum((e * gain).reshape(parts, 8, BLOCK), axis=0)
            inv = 1.0 / jnp.sum(total, axis=0, keepdims=True)
            delta = jnp.sum(mixed, axis=0, keepdims=True) * inv
            dqt = jnp.zeros((HEAD_SIZE, BLOCK), jnp.float32)
            for c in range(i + 1):
                keys = pl.ds(c * BLOCK, BLOCK)
                weight = scores[keys] * inv
                low = weight.astype(jnp.bfloat16)
                ds = (weight * (gains[keys] - delta)).astype(jnp.bfloat16)
                dv[keys] += dot(low, gb, ((1,), (0,)))
                dk[keys] += dot(ds, qb, ((1,), (0,)))
                dqt = dqt + dot(kt[:, keys], ds, ((1,), (0,)))
            keep_rows(dqs, i * BLOCK, turn(dqt.T * scale, at, -1.0).astype(jnp.bfloat16))
        parcel = parcels.at[h]
        for b in range(spans):
            parcel[pl.ds(b * span, span)] = dqs[order[b]]
        column = pl.multiple_of((me * GROUP + h) * HEAD_SIZE, HEAD_SIZE)
        scatter(parcel, dq_out.at[:, pl.ds(column, HEAD_SIZE)], 0)
        return carry

    lax.fori_loop(0, GROUP, head, 0)
    for b in range(spans):
        at = pl.ds(b * span, span)
        dqs[b] = turn(dk[at] * scale, at, -1.0).astype(jnp.bfloat16)
        dvs[b] = dv[at].astype(jnp.bfloat16)
    for b in range(spans):
        parcel_k[pl.ds(b * span, span)] = dqs[order[b]]
        parcel_v[pl.ds(b * span, span)] = dvs[order[b]]
    column = pl.ds(pl.multiple_of(me * HEAD_SIZE, HEAD_SIZE), HEAD_SIZE)
    scatter(parcel_k, dk_out.at[:, column], 1)
    scatter(parcel_v, dv_out.at[:, column], 2)
    away = HEAD_SIZE * (seq - 1)
    for sem in (send, recv):
        wait_bytes(dq_out.at[:, pl.ds(0, GROUP * away)], sem.at[0])
        wait_bytes(dk_out.at[:, pl.ds(0, away)], sem.at[1])
        wait_bytes(dv_out.at[:, pl.ds(0, away)], sem.at[2])
    wait_bytes(dq_out.at[:, pl.ds(0, GROUP * HEAD_SIZE)], own.at[0])
    wait_bytes(dk_out.at[:, pl.ds(0, HEAD_SIZE)], own.at[1])
    wait_bytes(dv_out.at[:, pl.ds(0, HEAD_SIZE)], own.at[2])


def attend(seq, order, inverse, q_all, k_all, v_all, g_all):
    tokens = k_all.shape[0]
    rows = tokens // seq
    span = tokens // order.shape[0]
    smem = pl.BlockSpec(memory_space=pltpu.SMEM)
    vmem = pl.BlockSpec(memory_space=pltpu.VMEM)
    hbm = pl.BlockSpec(memory_space=pl.ANY)
    table = jnp.asarray(rotary_table(tokens))
    low = jnp.bfloat16
    thin = (tokens, HEAD_SIZE)
    tall = (tokens, BLOCK)
    return pl.pallas_call(
        functools.partial(attend_kernel, seq, span),
        out_shape=(
            jax.ShapeDtypeStruct((rows, seq * q_all.shape[1]), low),
            jax.ShapeDtypeStruct((rows, seq * HEAD_SIZE), low),
            jax.ShapeDtypeStruct((rows, seq * HEAD_SIZE), low),
        ),
        in_specs=[smem, smem] + [vmem] * 5,
        out_specs=(hbm,) * 3,
        scratch_shapes=[
            pltpu.VMEM(thin, jnp.float32),
            pltpu.VMEM(thin, jnp.float32),
            pltpu.VMEM(thin, low),
            pltpu.VMEM(thin, low),
            pltpu.VMEM(thin, low),
            pltpu.VMEM(thin, low),
            pltpu.VMEM((HEAD_SIZE, tokens), low),
            pltpu.VMEM(thin, jnp.float32),
            pltpu.VMEM(thin, jnp.float32),
            pltpu.VMEM(tall, jnp.float32),
            pltpu.VMEM(tall, jnp.float32),
            pltpu.VMEM((tokens // span, span, HEAD_SIZE), low),
            pltpu.VMEM((tokens // span, span, HEAD_SIZE), low),
            pltpu.VMEM((GROUP,) + thin, low),
            pltpu.VMEM(thin, low),
            pltpu.VMEM(thin, low),
            pltpu.SemaphoreType.DMA((3,)),
            pltpu.SemaphoreType.DMA((3,)),
            pltpu.SemaphoreType.DMA((3,)),
        ],
        compiler_params=pltpu.CompilerParams(
            collective_id=0, has_side_effects=True, vmem_limit_bytes=56 << 20
        ),
        name="attend",
    )(order, inverse, *(a.reshape(-1, span, a.shape[1]) for a in (q_all, k_all, v_all, g_all)), table)


def body(sections, seq, q, k, v, g, partner, order):
    span_index = jnp.arange(order.shape[0], dtype=jnp.int32)
    inverse = jnp.sum(
        jnp.where(order[:, None] == span_index[None, :], span_index[:, None], 0), axis=0
    )
    branches = [functools.partial(gather, pair, seq) for pair in range(1, sections)]
    moved = lax.switch(partner[0] - 1, branches, q[0, 0], k[0, 0], v[0, 0], g[0, 0])
    results = attend(seq, order, inverse, *moved)
    return tuple(result[None, None] for result in results)


def solution(mesh):
    placed = P("section", None, "seq", None)
    return jax.shard_map(
        functools.partial(body, mesh.shape["section"], mesh.shape["seq"]),
        mesh=mesh,
        in_specs=(placed, placed, placed, placed, P(), P()),
        out_specs=(placed, placed, placed),
        check_vma=False,
    )
```

```python
import functools
import math

import jax
import jax.numpy as jnp
import numpy as np
from jax import lax
from jax.experimental import pallas as pl
from jax.experimental.pallas import tpu as pltpu
from jax.sharding import PartitionSpec as P

QUERY_HEADS = 64
KEY_VALUE_HEADS = 8
HEAD_SIZE = 128
GROUP = QUERY_HEADS // KEY_VALUE_HEADS
BLOCK = 256
CHUNK = 128
UNIT = 1
MESH = pl.DeviceIdType.MESH
MIXED = ((1, 0), (3, 0), (0, 1), (2, 0), (1, 1), (3, 1), (2, 1), (0, 0))


def rotary_table(tokens):
    half = HEAD_SIZE // 2
    steps = np.arange(0, HEAD_SIZE, 2).astype(np.float32) / np.float32(HEAD_SIZE)
    frequency = np.power(np.float32(1000000.0), -steps).astype(np.float32)
    angles = np.arange(tokens, dtype=np.float32)[:, None] * frequency[None, :]
    angles = angles.astype(np.float64)
    table = np.concatenate([np.cos(angles), np.sin(angles)], axis=1).astype(np.float32)
    assert table.shape == (tokens, 2 * half)
    return table


def xor_static(index, mask):
    result = index
    bit = 1
    while bit <= mask:
        if mask & bit:
            low = lax.rem(lax.div(index, bit), 2)
            result = result + (1 - 2 * low) * bit
        bit *= 2
    return result


def wait_bytes(like, sem):
    pltpu.make_async_copy(like, like, sem).wait()


def wait_own(like, sem):
    pltpu.make_async_copy(like, like, sem).wait()


def peer(me, seq, dx, dz):
    lines = seq // 2
    return lax.rem(lax.div(me, 2) + dx, lines) * 2 + lax.rem(lax.rem(me, 2) + dz, 2)


def gather_kernel(pair, seq, q_ref, k_ref, v_ref, g_ref, q_all, k_all, v_all, g_all, send, recv, own):
    section = lax.axis_index("section")
    me = lax.axis_index("seq")
    other = xor_static(section, pair)
    rows = q_ref.shape[0]
    targets = [(peer(me, seq, dx, dz), dx or dz) for dx, dz in MIXED]
    barrier = pltpu.get_barrier_semaphore()
    for to, away in targets:
        pl.semaphore_signal(
            barrier, inc=1, device_id={"section": other, "seq": to}, device_id_type=MESH
        )
        if away:
            pl.semaphore_signal(
                barrier, inc=1, device_id={"section": section, "seq": to}, device_id_type=MESH
            )
    pl.semaphore_wait(barrier, 2 * seq - 1)
    mine = pl.ds(pl.multiple_of(me * rows, rows), rows)

    def column(block):
        return pl.ds(pl.multiple_of(block * HEAD_SIZE, HEAD_SIZE), HEAD_SIZE)

    def send_to(source, to, target, index, device):
        pltpu.make_async_remote_copy(
            src_ref=source,
            dst_ref=target,
            send_sem=send.at[index],
            recv_sem=recv.at[index],
            device_id={"section": device, "seq": to},
            device_id_type=MESH,
        ).start()

    def step(h, carry):
        for to, away in targets:
            wide = column(to * GROUP + h)
            send_to(q_ref.at[:, wide], to, q_all.at[h, mine], 2, other)
            if away:
                send_to(g_ref.at[:, wide], to, g_all.at[h, mine], 3, section)
        pltpu.make_async_copy(
            g_ref.at[:, column(me * GROUP + h)], g_all.at[h, mine], own
        ).start()
        return carry

    for to, _ in targets:
        send_to(k_ref.at[:, column(to)], to, k_all.at[mine], 0, other)
        send_to(v_ref.at[:, column(to)], to, v_all.at[mine], 1, other)
    lax.fori_loop(0, GROUP, step, 0)
    wait_own(g_all.at[:, pl.ds(0, rows)], own)
    shared = pl.ds(0, rows * (seq - 1))
    for sem in (send, recv):
        wait_bytes(k_all, sem.at[0])
        wait_bytes(v_all, sem.at[1])
        wait_bytes(q_all, sem.at[2])
        wait_bytes(g_all.at[:, shared], sem.at[3])


def gather(pair, seq, q, k, v, g):
    rows = q.shape[0]
    any_spec = pl.BlockSpec(memory_space=pl.ANY)
    thin = jax.ShapeDtypeStruct((rows * seq, HEAD_SIZE), q.dtype)
    wide = jax.ShapeDtypeStruct((GROUP, rows * seq, HEAD_SIZE), q.dtype)
    return pl.pallas_call(
        functools.partial(gather_kernel, pair, seq),
        out_shape=(wide, thin, thin, wide),
        in_specs=[any_spec] * 4,
        out_specs=(any_spec,) * 4,
        scratch_shapes=[
            pltpu.SemaphoreType.DMA((4,)),
            pltpu.SemaphoreType.DMA((4,)),
            pltpu.SemaphoreType.DMA(()),
        ],
        compiler_params=pltpu.CompilerParams(collective_id=pair, has_side_effects=True, vmem_limit_bytes=2 << 20),
        name=f"gather_{pair}",
    )(q, k, v, g)


def dot(a, b, dims):
    return lax.dot_general(a, b, (dims, ((), ())), preferred_element_type=jnp.float32)


def attend_kernel(
    seq,
    span,
    order,
    inverse,
    q_all,
    k_all,
    v_all,
    g_all,
    table,
    dq_out,
    dk_out,
    dv_out,
    cosine,
    sine,
    qs,
    ks,
    vs,
    gs,
    kt,
    dk,
    dv,
    scores,
    gains,
    dqs,
    dvs,
    parcels,
    parcel_k,
    parcel_v,
    send,
    recv,
    own,
):
    section = lax.axis_index("section")
    me = lax.axis_index("seq")
    spans = k_all.shape[0]
    tokens = spans * span
    rows = tokens // seq
    half = HEAD_SIZE // 2
    blocks = tokens // BLOCK
    scale = HEAD_SIZE**-0.5
    scale2 = scale * math.log2(math.e)
    barrier = pltpu.get_barrier_semaphore()
    for j in range(1, seq):
        pl.semaphore_signal(
            barrier,
            inc=1,
            device_id={"section": section, "seq": lax.rem(me + j, seq)},
            device_id_type=MESH,
        )
    pl.semaphore_wait(barrier, seq - 1)

    def turn(x, at, sign):
        return x * cosine[at] + sign * (pltpu.roll(x, half, 1) * sine[at])

    first = lax.broadcasted_iota(jnp.int32, (span, HEAD_SIZE), 1) < half
    for b in range(spans):
        at = pl.ds(b * span, span)
        both = table[at]
        swapped = pltpu.roll(both, half, 1)
        cosine[at] = jnp.where(first, both, swapped)
        sine[at] = jnp.where(first, -swapped, both)
        key = turn(k_all[inverse[b]].astype(jnp.float32), at, 1.0)
        ks[at] = key.astype(jnp.bfloat16)
        vs[at] = v_all[inverse[b]]
    kt[...] = ks[...].T
    dk[...] = jnp.zeros_like(dk)
    dv[...] = jnp.zeros_like(dv)
    diagonal = lax.broadcasted_iota(jnp.int32, (BLOCK, BLOCK), 0) <= lax.broadcasted_iota(
        jnp.int32, (BLOCK, BLOCK), 1
    )
    parts = BLOCK // 8

    def send_to(source, target, index, to):
        pltpu.make_async_remote_copy(
            src_ref=source.at[pl.ds(pl.multiple_of(to * rows, rows), rows)],
            dst_ref=target,
            send_sem=send.at[index],
            recv_sem=recv.at[index],
            device_id={"section": section, "seq": to},
            device_id_type=MESH,
        ).start()

    def scatter(source, target, index):
        for dx, dz in MIXED:
            if dx or dz:
                send_to(source, target, index, peer(me, seq, dx, dz))
        pltpu.make_async_copy(
            source.at[pl.ds(pl.multiple_of(me * rows, rows), rows)], target, own.at[index]
        ).start()

    def keep_rows(target, start, value):
        stop = start + value.shape[0]
        row = start
        while row < stop:
            b, low = row // span, row % span
            size = min(span - low, stop - row)
            target[b, pl.ds(low, size)] = value[row - start : row - start + size]
            row += size

    def group(step, carry):
        for u in range(UNIT):
            h = step * UNIT + u
            for b in range(spans):
                at = pl.ds(b * span, span)
                query = turn(q_all[h, inverse[b]].astype(jnp.float32), at, 1.0)
                qs[u, at] = query.astype(jnp.bfloat16)
                gs[u, at] = g_all[h, inverse[b]]

        def start(u, i):
            score, gain_keep = scores.at[i % 2, u], gains.at[i % 2, u]
            qb = qs[u, pl.ds(i * BLOCK, BLOCK)]
            gb = gs[u, pl.ds(i * BLOCK, BLOCK)]
            tops = []
            top = None
            for c in range((i + 1) * BLOCK // CHUNK):
                keys = pl.ds(c * CHUNK, CHUNK)
                s = dot(ks[keys], qb, ((1,), (1,)))
                low_key = c * CHUNK - i * BLOCK
                if low_key >= 0:
                    s = jnp.where(diagonal[low_key : low_key + CHUNK], s, -jnp.inf)
                gain = dot(vs[keys], gb, ((1,), (1,)))
                part = jnp.max(jnp.max(s.reshape(CHUNK // 8, 8, BLOCK), axis=0), axis=0, keepdims=True)
                new = part if top is None else jnp.maximum(top, part)
                e = jnp.exp2((s - new) * scale2)
                score[keys] = e
                gain_keep[keys] = gain
                tsum = jnp.sum(e.reshape(CHUNK // 8, 8, BLOCK), axis=0)
                msum = jnp.sum((e * gain).reshape(CHUNK // 8, 8, BLOCK), axis=0)
                if top is None:
                    total, mixed = tsum, msum
                else:
                    fade = jnp.exp2((top - new) * scale2)
                    total = total * fade + tsum
                    mixed = mixed * fade + msum
                top = new
                tops.append(new)
            inv = 1.0 / jnp.sum(total, axis=0, keepdims=True)
            delta = jnp.sum(mixed, axis=0, keepdims=True) * inv
            return [inv * jnp.exp2((t - top) * scale2) for t in tops], delta

        def finish(i, ready):
            at = pl.ds(i * BLOCK, BLOCK)
            qb = jnp.concatenate([qs[u, at] for u in range(UNIT)], axis=0)
            gb = jnp.concatenate([gs[u, at] for u in range(UNIT)], axis=0)
            dqt = [jnp.zeros((HEAD_SIZE, BLOCK), jnp.float32)] * UNIT
            for c in range(i + 1):
                keys = pl.ds(c * BLOCK, BLOCK)
                wide_low, wide_ds = [], []
                for u in range(UNIT):
                    invs, delta = ready[u]
                    lows, dss = [], []
                    for f in range(BLOCK // CHUNK):
                        sub = pl.ds(c * BLOCK + f * CHUNK, CHUNK)
                        weight = scores[i % 2, u, sub] * invs[c * (BLOCK // CHUNK) + f]
                        lows.append(weight.astype(jnp.bfloat16))
                        dss.append((weight * (gains[i % 2, u, sub] - delta)).astype(jnp.bfloat16))
                    wide_low.append(jnp.concatenate(lows, axis=0))
                    ds = jnp.concatenate(dss, axis=0)
                    wide_ds.append(ds)
                    dqt[u] = dqt[u] + dot(kt[:, keys], ds, ((1,), (0,)))
                dv[keys] += dot(jnp.concatenate(wide_low, axis=1), gb, ((1,), (0,)))
                dk[keys] += dot(jnp.concatenate(wide_ds, axis=1), qb, ((1,), (0,)))
            for u in range(UNIT):
                keep_rows(dqs.at[u], i * BLOCK, turn(dqt[u].T * scale, at, -1.0).astype(jnp.bfloat16))

        ready = [start(u, 0) for u in range(UNIT)]
        for i in range(blocks):
            now = ready
            if i + 1 < blocks:
                ready = [start(u, i + 1) for u in range(UNIT)]
            finish(i, now)
        for u in range(UNIT):
            h = step * UNIT + u
            parcel = parcels.at[h]
            for b in range(spans):
                parcel[pl.ds(b * span, span)] = dqs[u, order[b]]
            column = pl.multiple_of((me * GROUP + h) * HEAD_SIZE, HEAD_SIZE)
            scatter(parcel, dq_out.at[:, pl.ds(column, HEAD_SIZE)], 0)
        return carry

    lax.fori_loop(0, GROUP // UNIT, group, 0)
    for b in range(spans):
        at = pl.ds(b * span, span)
        dqs[0, b] = turn(dk[at] * scale, at, -1.0).astype(jnp.bfloat16)
        dvs[b] = dv[at].astype(jnp.bfloat16)
    for b in range(spans):
        parcel_k[pl.ds(b * span, span)] = dqs[0, order[b]]
        parcel_v[pl.ds(b * span, span)] = dvs[order[b]]
    column = pl.ds(pl.multiple_of(me * HEAD_SIZE, HEAD_SIZE), HEAD_SIZE)
    scatter(parcel_k, dk_out.at[:, column], 1)
    scatter(parcel_v, dv_out.at[:, column], 2)
    away = HEAD_SIZE * (seq - 1)
    for sem in (send, recv):
        wait_bytes(dq_out.at[:, pl.ds(0, GROUP * away)], sem.at[0])
        wait_bytes(dk_out.at[:, pl.ds(0, away)], sem.at[1])
        wait_bytes(dv_out.at[:, pl.ds(0, away)], sem.at[2])
    wait_own(dq_out.at[:, pl.ds(0, GROUP * HEAD_SIZE)], own.at[0])
    wait_own(dk_out.at[:, pl.ds(0, HEAD_SIZE)], own.at[1])
    wait_own(dv_out.at[:, pl.ds(0, HEAD_SIZE)], own.at[2])


def attend(seq, order, inverse, q_all, k_all, v_all, g_all):
    tokens = k_all.shape[0]
    rows = tokens // seq
    span = tokens // order.shape[0]
    smem = pl.BlockSpec(memory_space=pltpu.SMEM)
    vmem = pl.BlockSpec(memory_space=pltpu.VMEM)
    hbm = pl.BlockSpec(memory_space=pl.ANY)
    table = jnp.asarray(rotary_table(tokens))
    low = jnp.bfloat16
    thin = (tokens, HEAD_SIZE)
    tall = (tokens, BLOCK)
    return pl.pallas_call(
        functools.partial(attend_kernel, seq, span),
        out_shape=(
            jax.ShapeDtypeStruct((rows, seq * GROUP * HEAD_SIZE), low),
            jax.ShapeDtypeStruct((rows, seq * HEAD_SIZE), low),
            jax.ShapeDtypeStruct((rows, seq * HEAD_SIZE), low),
        ),
        in_specs=[smem, smem] + [vmem] * 5,
        out_specs=(hbm,) * 3,
        scratch_shapes=[
            pltpu.VMEM(thin, jnp.float32),
            pltpu.VMEM(thin, jnp.float32),
            pltpu.VMEM((UNIT,) + thin, low),
            pltpu.VMEM(thin, low),
            pltpu.VMEM(thin, low),
            pltpu.VMEM((UNIT,) + thin, low),
            pltpu.VMEM((HEAD_SIZE, tokens), low),
            pltpu.VMEM(thin, jnp.float32),
            pltpu.VMEM(thin, jnp.float32),
            pltpu.VMEM((2, UNIT) + tall, jnp.float32),
            pltpu.VMEM((2, UNIT) + tall, jnp.float32),
            pltpu.VMEM((UNIT, tokens // span, span, HEAD_SIZE), low),
            pltpu.VMEM((tokens // span, span, HEAD_SIZE), low),
            pltpu.VMEM((GROUP,) + thin, low),
            pltpu.VMEM(thin, low),
            pltpu.VMEM(thin, low),
            pltpu.SemaphoreType.DMA((3,)),
            pltpu.SemaphoreType.DMA((3,)),
            pltpu.SemaphoreType.DMA((3,)),
        ],
        compiler_params=pltpu.CompilerParams(
            collective_id=0, has_side_effects=True, vmem_limit_bytes=25 << 20
        ),
        name="attend",
    )(order, inverse, *(
        a.reshape(a.shape[:-2] + (-1, span, a.shape[-1])) for a in (q_all, k_all, v_all, g_all)
    ), table)


def body(sections, seq, q, k, v, g, partner, order):
    span_index = jnp.arange(order.shape[0], dtype=jnp.int32)
    inverse = jnp.sum(
        jnp.where(order[:, None] == span_index[None, :], span_index[:, None], 0), axis=0
    )
    branches = [functools.partial(gather, pair, seq) for pair in range(1, sections)]
    moved = lax.switch(partner[0] - 1, branches, q[0, 0], k[0, 0], v[0, 0], g[0, 0])
    results = attend(seq, order, inverse, *moved)
    return tuple(result[None, None] for result in results)


def solution(mesh):
    placed = P("section", None, "seq", None)
    return jax.shard_map(
        functools.partial(body, mesh.shape["section"], mesh.shape["seq"]),
        mesh=mesh,
        in_specs=(placed, placed, placed, placed, P(), P()),
        out_specs=(placed, placed, placed),
        check_vma=False,
    )
```

```python
import functools
import math

import jax
import jax.numpy as jnp
import numpy as np
from jax import lax
from jax.experimental import pallas as pl
from jax.experimental.pallas import tpu as pltpu
from jax.sharding import PartitionSpec as P

QUERY_HEADS = 64
KEY_VALUE_HEADS = 8
HEAD_SIZE = 128
GROUP = QUERY_HEADS // KEY_VALUE_HEADS
BLOCK = 256
CHUNK = 128
UNIT = 1
MESH = pl.DeviceIdType.MESH
MIXED = ((1, 0), (3, 0), (0, 1), (2, 0), (1, 1), (3, 1), (2, 1), (0, 0))


def rotary_table(tokens):
    half = HEAD_SIZE // 2
    steps = np.arange(0, HEAD_SIZE, 2).astype(np.float32) / np.float32(HEAD_SIZE)
    frequency = np.power(np.float32(1000000.0), -steps).astype(np.float32)
    angles = np.arange(tokens, dtype=np.float32)[:, None] * frequency[None, :]
    angles = angles.astype(np.float64)
    table = np.concatenate([np.cos(angles), np.sin(angles)], axis=1).astype(np.float32)
    assert table.shape == (tokens, 2 * half)
    return table


def xor_static(index, mask):
    result = index
    bit = 1
    while bit <= mask:
        if mask & bit:
            low = lax.rem(lax.div(index, bit), 2)
            result = result + (1 - 2 * low) * bit
        bit *= 2
    return result


def wait_bytes(like, sem):
    pltpu.make_async_copy(like, like, sem).wait()


def wait_own(like, sem):
    pltpu.make_async_copy(like, like, sem).wait()


def peer(me, seq, dx, dz):
    lines = seq // 2
    return lax.rem(lax.div(me, 2) + dx, lines) * 2 + lax.rem(lax.rem(me, 2) + dz, 2)


def gather_kernel(pair, seq, q_ref, k_ref, v_ref, g_ref, q_all, k_all, v_all, g_all, send, recv, own):
    section = lax.axis_index("section")
    me = lax.axis_index("seq")
    other = xor_static(section, pair)
    rows = q_ref.shape[0]
    targets = [(peer(me, seq, dx, dz), dx or dz) for dx, dz in MIXED]
    barrier = pltpu.get_barrier_semaphore()
    for to, away in targets:
        pl.semaphore_signal(
            barrier, inc=1, device_id={"section": other, "seq": to}, device_id_type=MESH
        )
        if away:
            pl.semaphore_signal(
                barrier, inc=1, device_id={"section": section, "seq": to}, device_id_type=MESH
            )
    pl.semaphore_wait(barrier, 2 * seq - 1)
    mine = pl.ds(pl.multiple_of(me * rows, rows), rows)

    def column(block):
        return pl.ds(pl.multiple_of(block * HEAD_SIZE, HEAD_SIZE), HEAD_SIZE)

    def send_to(source, to, target, index, device):
        pltpu.make_async_remote_copy(
            src_ref=source,
            dst_ref=target,
            send_sem=send.at[index],
            recv_sem=recv.at[index],
            device_id={"section": device, "seq": to},
            device_id_type=MESH,
        ).start()

    def step(h, carry):
        for to, away in targets:
            wide = column(to * GROUP + h)
            send_to(q_ref.at[:, wide], to, q_all.at[h, mine], 2, other)
            if away:
                send_to(g_ref.at[:, wide], to, g_all.at[h, mine], 3, section)
        pltpu.make_async_copy(
            g_ref.at[:, column(me * GROUP + h)], g_all.at[h, mine], own
        ).start()
        return carry

    for to, _ in targets:
        send_to(k_ref.at[:, column(to)], to, k_all.at[mine], 0, other)
        send_to(v_ref.at[:, column(to)], to, v_all.at[mine], 1, other)
    lax.fori_loop(0, GROUP, step, 0)
    wait_own(g_all.at[:, pl.ds(0, rows)], own)
    shared = pl.ds(0, rows * (seq - 1))
    for sem in (send, recv):
        wait_bytes(k_all, sem.at[0])
        wait_bytes(v_all, sem.at[1])
        wait_bytes(q_all, sem.at[2])
        wait_bytes(g_all.at[:, shared], sem.at[3])


def gather(pair, seq, q, k, v, g):
    rows = q.shape[0]
    any_spec = pl.BlockSpec(memory_space=pl.ANY)
    thin = jax.ShapeDtypeStruct((rows * seq, HEAD_SIZE), q.dtype)
    wide = jax.ShapeDtypeStruct((GROUP, rows * seq, HEAD_SIZE), q.dtype)
    return pl.pallas_call(
        functools.partial(gather_kernel, pair, seq),
        out_shape=(wide, thin, thin, wide),
        in_specs=[any_spec] * 4,
        out_specs=(any_spec,) * 4,
        scratch_shapes=[
            pltpu.SemaphoreType.DMA((4,)),
            pltpu.SemaphoreType.DMA((4,)),
            pltpu.SemaphoreType.DMA(()),
        ],
        compiler_params=pltpu.CompilerParams(collective_id=pair, has_side_effects=True, vmem_limit_bytes=2 << 20),
        name=f"gather_{pair}",
    )(q, k, v, g)


def beside(left, right):
    return right if left.shape[1] == 0 else jnp.concatenate([left, right], axis=1)


def dot(a, b, dims):
    return lax.dot_general(a, b, (dims, ((), ())), preferred_element_type=jnp.float32)


def attend_kernel(
    seq,
    span,
    order,
    inverse,
    q_all,
    k_all,
    v_all,
    g_all,
    table,
    dq_out,
    dk_out,
    dv_out,
    cosine,
    sine,
    qs,
    ks,
    vs,
    gs,
    kt,
    q_next,
    g_next,
    dk,
    dv,
    scores,
    gains,
    dqs,
    dvs,
    parcels,
    parcel_k,
    parcel_v,
    send,
    recv,
    own,
    load,
):
    section = lax.axis_index("section")
    me = lax.axis_index("seq")
    spans = k_all.shape[0]
    tokens = spans * span
    rows = tokens // seq
    half = HEAD_SIZE // 2
    blocks = tokens // BLOCK
    scale = HEAD_SIZE**-0.5
    scale2 = scale * math.log2(math.e)
    barrier = pltpu.get_barrier_semaphore()
    for j in range(1, seq):
        pl.semaphore_signal(
            barrier,
            inc=1,
            device_id={"section": section, "seq": lax.rem(me + j, seq)},
            device_id_type=MESH,
        )
    pl.semaphore_wait(barrier, seq - 1)

    def fetch(h):
        return (
            pltpu.make_async_copy(q_all.at[h], q_next, load.at[0]),
            pltpu.make_async_copy(g_all.at[h], g_next, load.at[1]),
        )

    for copy in fetch(0):
        copy.start()

    def turn(x, at, sign):
        return x * cosine[at] + sign * (pltpu.roll(x, half, 1) * sine[at])

    first = lax.broadcasted_iota(jnp.int32, (span, HEAD_SIZE), 1) < half
    for b in range(spans):
        at = pl.ds(b * span, span)
        both = table[at]
        swapped = pltpu.roll(both, half, 1)
        cosine[at] = jnp.where(first, both, swapped)
        sine[at] = jnp.where(first, -swapped, both)
        key = turn(k_all[inverse[b]].astype(jnp.float32), at, 1.0)
        ks[at] = key.astype(jnp.bfloat16)
        vs[at] = v_all[inverse[b]]
    kt[...] = ks[...].T
    dk[...] = jnp.zeros_like(dk)
    dv[...] = jnp.zeros_like(dv)
    diagonal = lax.broadcasted_iota(jnp.int32, (CHUNK, BLOCK), 0) <= lax.broadcasted_iota(
        jnp.int32, (CHUNK, BLOCK), 1
    )

    def send_to(source, target, index, to):
        pltpu.make_async_remote_copy(
            src_ref=source.at[pl.ds(pl.multiple_of(to * rows, rows), rows)],
            dst_ref=target,
            send_sem=send.at[index],
            recv_sem=recv.at[index],
            device_id={"section": section, "seq": to},
            device_id_type=MESH,
        ).start()

    def scatter(source, target, index):
        for dx, dz in MIXED:
            if dx or dz:
                send_to(source, target, index, peer(me, seq, dx, dz))
        pltpu.make_async_copy(
            source.at[pl.ds(pl.multiple_of(me * rows, rows), rows)], target, own.at[index]
        ).start()

    def keep_rows(target, start, value):
        stop = start + value.shape[0]
        row = start
        while row < stop:
            b, low = row // span, row % span
            size = min(span - low, stop - row)
            target[b, pl.ds(low, size)] = value[row - start : row - start + size]
            row += size

    def group(step, carry):
        for u in range(UNIT):
            h = step * UNIT + u
            for copy in fetch(h):
                copy.wait()
            for b in range(spans):
                at = pl.ds(b * span, span)
                query = turn(q_next[inverse[b]].astype(jnp.float32), at, 1.0)
                qs[u, at] = query.astype(jnp.bfloat16)
                gs[u, at] = g_next[inverse[b]]
            for copy in fetch(lax.rem(h + 1, GROUP)):
                copy.start()

        def start(u, i):
            score, gain_keep = scores.at[i % 2, u], gains.at[i % 2, u]
            qb = qs[u, pl.ds(i * BLOCK, BLOCK)]
            gb = gs[u, pl.ds(i * BLOCK, BLOCK)]
            tops = []
            top = None
            for c in range((i + 1) * BLOCK // CHUNK):
                keys = pl.ds(c * CHUNK, CHUNK)
                skip = max(c * CHUNK - i * BLOCK, 0)
                width = BLOCK - skip
                s = dot(ks[keys], qb[skip:], ((1,), (1,)))
                if c * CHUNK >= i * BLOCK:
                    s = jnp.where(diagonal[:, :width], s, -jnp.inf)
                gain = dot(vs[keys], gb[skip:], ((1,), (1,)))
                new = jnp.max(jnp.max(s.reshape(CHUNK // 8, 8, width), axis=0), axis=0, keepdims=True)
                if top is not None:
                    new = jnp.maximum(top[:, skip:], new)
                e = jnp.exp2((s - new) * scale2)
                score[keys, skip:] = e
                gain_keep[keys, skip:] = gain
                tsum = jnp.sum(e.reshape(CHUNK // 8, 8, width), axis=0)
                msum = jnp.sum((e * gain).reshape(CHUNK // 8, 8, width), axis=0)
                if top is None:
                    total, mixed = tsum, msum
                else:
                    fade = jnp.exp2((top[:, skip:] - new) * scale2)
                    tsum = total[:, skip:] * fade + tsum
                    msum = mixed[:, skip:] * fade + msum
                    total = beside(total[:, :skip], tsum)
                    mixed = beside(mixed[:, :skip], msum)
                    new = beside(top[:, :skip], new)
                top = new
                tops.append(new)
            inv = 1.0 / jnp.sum(total, axis=0, keepdims=True)
            delta = jnp.sum(mixed, axis=0, keepdims=True) * inv
            return [inv * jnp.exp2((t - top) * scale2) for t in tops], delta

        def finish(i, ready):
            at = pl.ds(i * BLOCK, BLOCK)
            qb = jnp.concatenate([qs[u, at] for u in range(UNIT)], axis=0)
            gb = jnp.concatenate([gs[u, at] for u in range(UNIT)], axis=0)
            dqt = [jnp.zeros((HEAD_SIZE, BLOCK), jnp.float32)] * UNIT
            for c in range(i + 1):
                keys = pl.ds(c * BLOCK, BLOCK)
                wide_low, wide_ds = [], []
                for u in range(UNIT):
                    invs, delta = ready[u]
                    lows, dss = [], []
                    for f in range(BLOCK // CHUNK):
                        sub = pl.ds(c * BLOCK + f * CHUNK, CHUNK)
                        skip = f * CHUNK if c == i else 0
                        none = jnp.zeros((CHUNK, skip), jnp.bfloat16)
                        weight = scores[i % 2, u, sub, skip:] * invs[c * (BLOCK // CHUNK) + f][:, skip:]
                        change = weight * (gains[i % 2, u, sub, skip:] - delta[:, skip:])
                        lows.append(beside(none, weight.astype(jnp.bfloat16)))
                        dss.append(beside(none, change.astype(jnp.bfloat16)))
                    wide_low.append(jnp.concatenate(lows, axis=0))
                    ds = jnp.concatenate(dss, axis=0)
                    wide_ds.append(ds)
                    dqt[u] = dqt[u] + dot(kt[:, keys], ds, ((1,), (0,)))
                dv[keys] += dot(jnp.concatenate(wide_low, axis=1), gb, ((1,), (0,)))
                dk[keys] += dot(jnp.concatenate(wide_ds, axis=1), qb, ((1,), (0,)))
            for u in range(UNIT):
                keep_rows(dqs.at[u], i * BLOCK, turn(dqt[u].T * scale, at, -1.0).astype(jnp.bfloat16))

        ready = [start(u, 0) for u in range(UNIT)]
        for i in range(blocks):
            now = ready
            if i + 1 < blocks:
                ready = [start(u, i + 1) for u in range(UNIT)]
            finish(i, now)
        for u in range(UNIT):
            h = step * UNIT + u
            parcel = parcels.at[h]
            for b in range(spans):
                parcel[pl.ds(b * span, span)] = dqs[u, order[b]]
            column = pl.multiple_of((me * GROUP + h) * HEAD_SIZE, HEAD_SIZE)
            scatter(parcel, dq_out.at[:, pl.ds(column, HEAD_SIZE)], 0)
        return carry

    lax.fori_loop(0, GROUP // UNIT, group, 0)
    for copy in fetch(0):
        copy.wait()
    for b in range(spans):
        at = pl.ds(b * span, span)
        dqs[0, b] = turn(dk[at] * scale, at, -1.0).astype(jnp.bfloat16)
        dvs[b] = dv[at].astype(jnp.bfloat16)
    for b in range(spans):
        parcel_k[pl.ds(b * span, span)] = dqs[0, order[b]]
        parcel_v[pl.ds(b * span, span)] = dvs[order[b]]
    column = pl.ds(pl.multiple_of(me * HEAD_SIZE, HEAD_SIZE), HEAD_SIZE)
    scatter(parcel_k, dk_out.at[:, column], 1)
    scatter(parcel_v, dv_out.at[:, column], 2)
    away = HEAD_SIZE * (seq - 1)
    for sem in (send, recv):
        wait_bytes(dq_out.at[:, pl.ds(0, GROUP * away)], sem.at[0])
        wait_bytes(dk_out.at[:, pl.ds(0, away)], sem.at[1])
        wait_bytes(dv_out.at[:, pl.ds(0, away)], sem.at[2])
    wait_own(dq_out.at[:, pl.ds(0, GROUP * HEAD_SIZE)], own.at[0])
    wait_own(dk_out.at[:, pl.ds(0, HEAD_SIZE)], own.at[1])
    wait_own(dv_out.at[:, pl.ds(0, HEAD_SIZE)], own.at[2])


def attend(seq, order, inverse, q_all, k_all, v_all, g_all):
    tokens = k_all.shape[0]
    rows = tokens // seq
    span = tokens // order.shape[0]
    smem = pl.BlockSpec(memory_space=pltpu.SMEM)
    vmem = pl.BlockSpec(memory_space=pltpu.VMEM)
    hbm = pl.BlockSpec(memory_space=pl.ANY)
    table = jnp.asarray(rotary_table(tokens))
    low = jnp.bfloat16
    thin = (tokens, HEAD_SIZE)
    tall = (tokens, BLOCK)
    return pl.pallas_call(
        functools.partial(attend_kernel, seq, span),
        out_shape=(
            jax.ShapeDtypeStruct((rows, seq * GROUP * HEAD_SIZE), low),
            jax.ShapeDtypeStruct((rows, seq * HEAD_SIZE), low),
            jax.ShapeDtypeStruct((rows, seq * HEAD_SIZE), low),
        ),
        in_specs=[smem, smem, hbm, vmem, vmem, hbm, vmem],
        out_specs=(hbm,) * 3,
        scratch_shapes=[
            pltpu.VMEM(thin, jnp.float32),
            pltpu.VMEM(thin, jnp.float32),
            pltpu.VMEM((UNIT,) + thin, low),
            pltpu.VMEM(thin, low),
            pltpu.VMEM(thin, low),
            pltpu.VMEM((UNIT,) + thin, low),
            pltpu.VMEM((HEAD_SIZE, tokens), low),
            pltpu.VMEM((tokens // span, span, HEAD_SIZE), low),
            pltpu.VMEM((tokens // span, span, HEAD_SIZE), low),
            pltpu.VMEM(thin, jnp.float32),
            pltpu.VMEM(thin, jnp.float32),
            pltpu.VMEM((2, UNIT) + tall, jnp.float32),
            pltpu.VMEM((2, UNIT) + tall, jnp.float32),
            pltpu.VMEM((UNIT, tokens // span, span, HEAD_SIZE), low),
            pltpu.VMEM((tokens // span, span, HEAD_SIZE), low),
            pltpu.VMEM((GROUP,) + thin, low),
            pltpu.VMEM(thin, low),
            pltpu.VMEM(thin, low),
            pltpu.SemaphoreType.DMA((3,)),
            pltpu.SemaphoreType.DMA((3,)),
            pltpu.SemaphoreType.DMA((3,)),
            pltpu.SemaphoreType.DMA((2,)),
        ],
        compiler_params=pltpu.CompilerParams(
            collective_id=0, has_side_effects=True, vmem_limit_bytes=25 << 20
        ),
        name="attend",
    )(order, inverse, *(
        a.reshape(a.shape[:-2] + (-1, span, a.shape[-1])) for a in (q_all, k_all, v_all, g_all)
    ), table)


def store_kernel(*refs):
    sources, targets, sem = refs[:3], refs[3:6], refs[6]
    copies = [
        pltpu.make_async_copy(source, target, sem.at[index])
        for index, (source, target) in enumerate(zip(sources, targets))
    ]
    for copy in copies:
        copy.start()
    for copy in copies:
        copy.wait()


def store(results):
    any_spec = pl.BlockSpec(memory_space=pl.ANY)
    return pl.pallas_call(
        store_kernel,
        out_shape=tuple(jax.ShapeDtypeStruct(a.shape, a.dtype) for a in results),
        in_specs=[any_spec] * 3,
        out_specs=(any_spec,) * 3,
        scratch_shapes=[pltpu.SemaphoreType.DMA((3,))],
        compiler_params=pltpu.CompilerParams(vmem_limit_bytes=2 << 20),
        name="store",
    )(*results)


def body(sections, seq, q, k, v, g, partner, order):
    span_index = jnp.arange(order.shape[0], dtype=jnp.int32)
    inverse = jnp.sum(
        jnp.where(order[:, None] == span_index[None, :], span_index[:, None], 0), axis=0
    )
    branches = [functools.partial(gather, pair, seq) for pair in range(1, sections)]
    moved = lax.switch(partner[0] - 1, branches, q[0, 0], k[0, 0], v[0, 0], g[0, 0])
    results = attend(seq, order, inverse, *moved)
    return tuple(result[None, None] for result in store(results))


def solution(mesh):
    placed = P("section", None, "seq", None)
    return jax.shard_map(
        functools.partial(body, mesh.shape["section"], mesh.shape["seq"]),
        mesh=mesh,
        in_specs=(placed, placed, placed, placed, P(), P()),
        out_specs=(placed, placed, placed),
        check_vma=False,
    )
```

```python
import functools
import math

import jax
import jax.numpy as jnp
import numpy as np
from jax import lax
from jax.experimental import pallas as pl
from jax.experimental.pallas import tpu as pltpu
from jax.sharding import PartitionSpec as P

QUERY_HEADS = 64
KEY_VALUE_HEADS = 8
HEAD_SIZE = 128
GROUP = QUERY_HEADS // KEY_VALUE_HEADS
BLOCK = 256
CHUNK = 128
UNIT = 1
EARLY = 2
LATE = GROUP - EARLY
MESH = pl.DeviceIdType.MESH
MIXED = ((1, 0), (3, 0), (0, 1), (2, 0), (1, 1), (3, 1), (2, 1), (0, 0))


def rotary_table(tokens):
    half = HEAD_SIZE // 2
    steps = np.arange(0, HEAD_SIZE, 2).astype(np.float32) / np.float32(HEAD_SIZE)
    frequency = np.power(np.float32(1000000.0), -steps).astype(np.float32)
    angles = np.arange(tokens, dtype=np.float32)[:, None] * frequency[None, :]
    angles = angles.astype(np.float64)
    table = np.concatenate([np.cos(angles), np.sin(angles)], axis=1).astype(np.float32)
    assert table.shape == (tokens, 2 * half)
    return table


def xor_static(index, mask):
    result = index
    bit = 1
    while bit <= mask:
        if mask & bit:
            low = lax.rem(lax.div(index, bit), 2)
            result = result + (1 - 2 * low) * bit
        bit *= 2
    return result


def wait_bytes(like, sem):
    pltpu.make_async_copy(like, like, sem).wait()


def wait_own(like, sem):
    pltpu.make_async_copy(like, like, sem).wait()


def peer(me, seq, dx, dz):
    lines = seq // 2
    return lax.rem(lax.div(me, 2) + dx, lines) * 2 + lax.rem(lax.rem(me, 2) + dz, 2)


def beside(left, right):
    return right if left.shape[1] == 0 else jnp.concatenate([left, right], axis=1)


def dot(a, b, dims):
    return lax.dot_general(a, b, (dims, ((), ())), preferred_element_type=jnp.float32)


def turn(work, x, at, sign):
    return x * work["cosine"][at] + sign * (pltpu.roll(x, HEAD_SIZE // 2, 1) * work["sine"][at])


def prepare_tables(work, table, span, spans):
    first = lax.broadcasted_iota(jnp.int32, (span, HEAD_SIZE), 1) < HEAD_SIZE // 2

    def step(b, carry):
        at = pl.ds(pl.multiple_of(b * span, span), span)
        both = table[at]
        swapped = pltpu.roll(both, HEAD_SIZE // 2, 1)
        work["cosine"][at] = jnp.where(first, both, swapped)
        work["sine"][at] = jnp.where(first, -swapped, both)
        return carry

    lax.fori_loop(0, spans, step, 0)


def compact_head(work, span, spans, order, inverse, query_of, grad_of, parcel):
    qs, gs, ks, vs, kt = (work[name] for name in ("qs", "gs", "ks", "vs", "kt"))
    scores, gains, tops, dq = (work[name] for name in ("scores", "gains", "tops", "dq"))
    dk, dv, dqs = work["dk"], work["dv"], work["dqs"]
    scale = HEAD_SIZE**-0.5
    scale2 = scale * math.log2(math.e)
    parts = BLOCK // CHUNK
    rows = lax.broadcasted_iota(jnp.int32, (CHUNK, BLOCK), 0)
    lanes = lax.broadcasted_iota(jnp.int32, (CHUNK, BLOCK), 1)

    def sort(b, carry):
        at = pl.ds(pl.multiple_of(b * span, span), span)
        query = turn(work, query_of(inverse[b]).astype(jnp.float32), at, 1.0)
        qs[at] = query.astype(jnp.bfloat16)
        gs[at] = grad_of(inverse[b])
        return carry

    lax.fori_loop(0, spans, sort, 0)

    def block(i, carry):
        at = pl.ds(pl.multiple_of(i * BLOCK, BLOCK), BLOCK)

        def score(c, state, mask):
            top, total, mixed = state
            keys = pl.ds(pl.multiple_of(c * CHUNK, CHUNK), CHUNK)
            s = dot(ks[keys], qs[at], ((1,), (1,)))
            if mask is not None:
                s = jnp.where(rows + mask <= lanes, s, -jnp.inf)
            gain = dot(vs[keys], gs[at], ((1,), (1,)))
            new = jnp.max(jnp.max(s.reshape(CHUNK // 8, 8, BLOCK), axis=0), axis=0, keepdims=True)
            new = jnp.maximum(top, new)
            e = jnp.exp2((s - new) * scale2)
            scores[keys] = e
            gains[keys] = gain
            tops[c] = new
            fade = jnp.exp2((top - new) * scale2)
            total = total * fade + jnp.sum(e.reshape(CHUNK // 8, 8, BLOCK), axis=0)
            mixed = mixed * fade + jnp.sum((e * gain).reshape(CHUNK // 8, 8, BLOCK), axis=0)
            return new, total, mixed

        empty = jnp.zeros((8, BLOCK), jnp.float32)
        state = score(i * parts, (jnp.full((1, BLOCK), -jnp.inf), empty, empty), 0)
        for f in range(1, parts):
            state = score(i * parts + f, state, f * CHUNK)
        top, total, mixed = lax.fori_loop(
            0, i * parts, lambda c, now: score(c, now, None), state
        )
        inv = 1.0 / jnp.sum(total, axis=0, keepdims=True)
        delta = jnp.sum(mixed, axis=0, keepdims=True) * inv
        dq[...] = jnp.zeros_like(dq)

        def finish(c, carry):
            keys = pl.ds(pl.multiple_of(c * BLOCK, BLOCK), BLOCK)
            lows, dss = [], []
            for f in range(parts):
                sub = pl.ds(pl.multiple_of(c * BLOCK + f * CHUNK, CHUNK), CHUNK)
                factor = inv * jnp.exp2((tops[c * parts + f] - top) * scale2)
                weight = scores[sub] * factor
                lows.append(weight.astype(jnp.bfloat16))
                dss.append((weight * (gains[sub] - delta)).astype(jnp.bfloat16))
            low = jnp.concatenate(lows, axis=0)
            ds = jnp.concatenate(dss, axis=0)
            dv[keys] += dot(low, gs[at], ((1,), (0,)))
            dk[keys] += dot(ds, qs[at], ((1,), (0,)))
            dq[...] += dot(kt[:, keys], ds, ((1,), (0,)))
            return carry

        lax.fori_loop(0, i + 1, finish, 0)
        qs[at] = turn(work, dq[...].T * scale, at, -1.0).astype(jnp.bfloat16)
        return carry

    lax.fori_loop(0, spans * span // BLOCK, block, 0)

    def split(b, carry):
        dqs[b] = qs[pl.ds(pl.multiple_of(b * span, span), span)]
        return carry

    lax.fori_loop(0, spans, split, 0)

    def unsort(b, carry):
        parcel[pl.ds(pl.multiple_of(b * span, span), span)] = dqs[order[b]]
        return carry

    lax.fori_loop(0, spans, unsort, 0)


def gather_kernel(
    pair,
    seq,
    order,
    inverse,
    q_ref,
    k_ref,
    v_ref,
    g_ref,
    table_ref,
    q_late,
    g_late,
    ks,
    vs,
    dk,
    dv,
    parcels,
    q_early,
    g_early,
    k_land,
    v_land,
    table,
    cosine,
    sine,
    qs,
    gs,
    kt,
    scores,
    gains,
    tops,
    dq,
    dqs,
    send,
    recv,
    own,
):
    section = lax.axis_index("section")
    me = lax.axis_index("seq")
    other = xor_static(section, pair)
    held, span = q_ref.shape[:2]
    spans = held * seq
    targets = [(peer(me, seq, dx, dz), dx or dz) for dx, dz in MIXED]
    load = pltpu.make_async_copy(table_ref, table, own.at[2])
    load.start()
    barrier = pltpu.get_barrier_semaphore()
    for to, away in targets:
        pl.semaphore_signal(
            barrier, inc=1, device_id={"section": other, "seq": to}, device_id_type=MESH
        )
        if away:
            pl.semaphore_signal(
                barrier, inc=1, device_id={"section": section, "seq": to}, device_id_type=MESH
            )
    pl.semaphore_wait(barrier, 2 * seq - 1)
    mine = pl.ds(me * held, held)

    def column(block):
        return pl.ds(pl.multiple_of(block * HEAD_SIZE, HEAD_SIZE), HEAD_SIZE)

    def send_to(source, to, target, index, device):
        pltpu.make_async_remote_copy(
            src_ref=source,
            dst_ref=target,
            send_sem=send.at[index],
            recv_sem=recv.at[index],
            device_id={"section": device, "seq": to},
            device_id_type=MESH,
        ).start()

    def ship(first, count, q_target, g_target, index, local):
        def step(h, carry):
            for to, away in targets:
                wide = column(to * GROUP + first + h)
                send_to(q_ref.at[:, :, wide], to, q_target.at[h, mine], index, other)
                if away:
                    send_to(g_ref.at[:, :, wide], to, g_target.at[h, mine], index + 1, section)
            pltpu.make_async_copy(
                g_ref.at[:, :, column(me * GROUP + first + h)],
                g_target.at[h, mine],
                own.at[local],
            ).start()
            return carry

        lax.fori_loop(0, count, step, 0)

    for to, _ in targets:
        send_to(k_ref.at[:, :, column(to)], to, k_land.at[mine], 0, other)
        send_to(v_ref.at[:, :, column(to)], to, v_land.at[mine], 1, other)
    ship(0, EARLY, q_early, g_early, 2, 0)
    ship(EARLY, LATE, q_late, g_late, 4, 1)
    work = dict(
        cosine=cosine,
        sine=sine,
        qs=qs,
        gs=gs,
        ks=ks,
        vs=vs,
        kt=kt,
        scores=scores,
        gains=gains,
        tops=tops,
        dq=dq,
        dk=dk,
        dv=dv,
        dqs=dqs,
    )
    load.wait()
    prepare_tables(work, table, span, spans)
    dk[...] = jnp.zeros_like(dk)
    dv[...] = jnp.zeros_like(dv)
    others = pl.ds(0, spans - held)
    wait_bytes(k_land, recv.at[0])
    wait_bytes(v_land, recv.at[1])

    def place(b, carry):
        at = pl.ds(pl.multiple_of(b * span, span), span)
        key = turn(work, k_land[inverse[b]].astype(jnp.float32), at, 1.0)
        ks[at] = key.astype(jnp.bfloat16)
        vs[at] = v_land[inverse[b]]
        return carry

    lax.fori_loop(0, spans, place, 0)
    kt[...] = ks[...].T
    wait_bytes(q_early, recv.at[2])
    wait_bytes(g_early.at[:, others], recv.at[3])
    wait_own(g_early.at[:, pl.ds(0, held)], own.at[0])

    def head(h, carry):
        compact_head(
            work,
            span,
            spans,
            order,
            inverse,
            lambda b: q_early[h, b],
            lambda b: g_early[h, b],
            parcels.at[h],
        )
        return carry

    lax.fori_loop(0, EARLY, head, 0)
    wait_own(g_late.at[:, pl.ds(0, held)], own.at[1])
    wait_bytes(q_late, recv.at[4])
    wait_bytes(g_late.at[:, others], recv.at[5])
    wait_bytes(k_land, send.at[0])
    wait_bytes(v_land, send.at[1])
    wait_bytes(q_early, send.at[2])
    wait_bytes(g_early.at[:, others], send.at[3])
    wait_bytes(q_late, send.at[4])
    wait_bytes(g_late.at[:, others], send.at[5])


def gather(pair, seq, order, inverse, q, k, v, g, table):
    held, span = q.shape[:2]
    tokens = held * span * seq
    smem = pl.BlockSpec(memory_space=pltpu.SMEM)
    vmem = pl.BlockSpec(memory_space=pltpu.VMEM)
    hbm = pl.BlockSpec(memory_space=pl.ANY)
    low = jnp.bfloat16
    thin = (tokens, HEAD_SIZE)
    blocks = (held * seq, span, HEAD_SIZE)
    late = jax.ShapeDtypeStruct((LATE,) + blocks, low)
    return pl.pallas_call(
        functools.partial(gather_kernel, pair, seq),
        out_shape=(
            late,
            late,
            jax.ShapeDtypeStruct(thin, low),
            jax.ShapeDtypeStruct(thin, low),
            jax.ShapeDtypeStruct(thin, jnp.float32),
            jax.ShapeDtypeStruct(thin, jnp.float32),
            jax.ShapeDtypeStruct((EARLY,) + thin, low),
        ),
        in_specs=[smem, smem] + [hbm] * 5,
        out_specs=(hbm, hbm) + (vmem,) * 5,
        scratch_shapes=[
            pltpu.VMEM((EARLY,) + blocks, low),
            pltpu.VMEM((EARLY,) + blocks, low),
            pltpu.VMEM(blocks, low),
            pltpu.VMEM(blocks, low),
            pltpu.VMEM(thin, jnp.float32),
            pltpu.VMEM(thin, jnp.float32),
            pltpu.VMEM(thin, jnp.float32),
            pltpu.VMEM(thin, low),
            pltpu.VMEM(thin, low),
            pltpu.VMEM((HEAD_SIZE, tokens), low),
            pltpu.VMEM((tokens, BLOCK), jnp.float32),
            pltpu.VMEM((tokens, BLOCK), jnp.float32),
            pltpu.VMEM((tokens // CHUNK, 1, BLOCK), jnp.float32),
            pltpu.VMEM((HEAD_SIZE, BLOCK), jnp.float32),
            pltpu.VMEM(blocks, low),
            pltpu.SemaphoreType.DMA((6,)),
            pltpu.SemaphoreType.DMA((6,)),
            pltpu.SemaphoreType.DMA((3,)),
        ],
        compiler_params=pltpu.CompilerParams(
            collective_id=pair, has_side_effects=True, vmem_limit_bytes=20 << 20
        ),
        name=f"gather_{pair}",
    )(order, inverse, q, k, v, g, table)


def attend_kernel(
    seq,
    span,
    order,
    inverse,
    q_all,
    ks,
    vs,
    g_all,
    table,
    dk_start,
    dv_start,
    early,
    dq_out,
    dk_out,
    dv_out,
    cosine,
    sine,
    qs,
    gs,
    kt,
    q_next,
    g_next,
    dk,
    dv,
    scores,
    gains,
    dqs,
    dvs,
    parcels,
    parcel_k,
    parcel_v,
    send,
    recv,
    own,
    load,
):
    section = lax.axis_index("section")
    me = lax.axis_index("seq")
    tokens = ks.shape[0]
    spans = tokens // span
    rows = tokens // seq
    half = HEAD_SIZE // 2
    blocks = tokens // BLOCK
    scale = HEAD_SIZE**-0.5
    scale2 = scale * math.log2(math.e)
    barrier = pltpu.get_barrier_semaphore()
    for j in range(1, seq):
        pl.semaphore_signal(
            barrier,
            inc=1,
            device_id={"section": section, "seq": lax.rem(me + j, seq)},
            device_id_type=MESH,
        )
    pl.semaphore_wait(barrier, seq - 1)

    def fetch(h):
        return (
            pltpu.make_async_copy(q_all.at[h], q_next, load.at[0]),
            pltpu.make_async_copy(g_all.at[h], g_next, load.at[1]),
        )

    for copy in fetch(0):
        copy.start()

    def spin(x, at, sign):
        return x * cosine[at] + sign * (pltpu.roll(x, half, 1) * sine[at])

    prepare_tables({"cosine": cosine, "sine": sine}, table, span, spans)
    kt[...] = ks[...].T
    dk[...] = dk_start[...]
    dv[...] = dv_start[...]
    diagonal = lax.broadcasted_iota(jnp.int32, (CHUNK, BLOCK), 0) <= lax.broadcasted_iota(
        jnp.int32, (CHUNK, BLOCK), 1
    )

    def send_to(source, target, index, to):
        pltpu.make_async_remote_copy(
            src_ref=source.at[pl.ds(pl.multiple_of(to * rows, rows), rows)],
            dst_ref=target,
            send_sem=send.at[index],
            recv_sem=recv.at[index],
            device_id={"section": section, "seq": to},
            device_id_type=MESH,
        ).start()

    def scatter(source, target, index):
        for dx, dz in MIXED:
            if dx or dz:
                send_to(source, target, index, peer(me, seq, dx, dz))
        pltpu.make_async_copy(
            source.at[pl.ds(pl.multiple_of(me * rows, rows), rows)], target, own.at[index]
        ).start()

    for h in range(EARLY):
        column = pl.multiple_of((me * GROUP + h) * HEAD_SIZE, HEAD_SIZE)
        scatter(early.at[h], dq_out.at[:, pl.ds(column, HEAD_SIZE)], 0)

    def keep_rows(target, start, value):
        stop = start + value.shape[0]
        row = start
        while row < stop:
            b, low = row // span, row % span
            size = min(span - low, stop - row)
            target[b, pl.ds(low, size)] = value[row - start : row - start + size]
            row += size

    def group(step, carry):
        for u in range(UNIT):
            h = step * UNIT + u
            for copy in fetch(h):
                copy.wait()
            for b in range(spans):
                at = pl.ds(b * span, span)
                query = spin(q_next[inverse[b]].astype(jnp.float32), at, 1.0)
                qs[u, at] = query.astype(jnp.bfloat16)
                gs[u, at] = g_next[inverse[b]]
            for copy in fetch(lax.rem(h + 1, LATE)):
                copy.start()

        def start(u, i):
            score, gain_keep = scores.at[i % 2, u], gains.at[i % 2, u]
            qb = qs[u, pl.ds(i * BLOCK, BLOCK)]
            gb = gs[u, pl.ds(i * BLOCK, BLOCK)]
            tops = []
            top = None
            for c in range((i + 1) * BLOCK // CHUNK):
                keys = pl.ds(c * CHUNK, CHUNK)
                skip = max(c * CHUNK - i * BLOCK, 0)
                width = BLOCK - skip
                s = dot(ks[keys], qb[skip:], ((1,), (1,)))
                if c * CHUNK >= i * BLOCK:
                    s = jnp.where(diagonal[:, :width], s, -jnp.inf)
                gain = dot(vs[keys], gb[skip:], ((1,), (1,)))
                new = jnp.max(jnp.max(s.reshape(CHUNK // 8, 8, width), axis=0), axis=0, keepdims=True)
                if top is not None:
                    new = jnp.maximum(top[:, skip:], new)
                e = jnp.exp2((s - new) * scale2)
                score[keys, skip:] = e
                gain_keep[keys, skip:] = gain
                tsum = jnp.sum(e.reshape(CHUNK // 8, 8, width), axis=0)
                msum = jnp.sum((e * gain).reshape(CHUNK // 8, 8, width), axis=0)
                if top is None:
                    total, mixed = tsum, msum
                else:
                    fade = jnp.exp2((top[:, skip:] - new) * scale2)
                    tsum = total[:, skip:] * fade + tsum
                    msum = mixed[:, skip:] * fade + msum
                    total = beside(total[:, :skip], tsum)
                    mixed = beside(mixed[:, :skip], msum)
                    new = beside(top[:, :skip], new)
                top = new
                tops.append(new)
            inv = 1.0 / jnp.sum(total, axis=0, keepdims=True)
            delta = jnp.sum(mixed, axis=0, keepdims=True) * inv
            return [inv * jnp.exp2((t - top) * scale2) for t in tops], delta

        def finish(i, ready):
            at = pl.ds(i * BLOCK, BLOCK)
            qb = jnp.concatenate([qs[u, at] for u in range(UNIT)], axis=0)
            gb = jnp.concatenate([gs[u, at] for u in range(UNIT)], axis=0)
            dqt = [jnp.zeros((HEAD_SIZE, BLOCK), jnp.float32)] * UNIT
            for c in range(i + 1):
                keys = pl.ds(c * BLOCK, BLOCK)
                wide_low, wide_ds = [], []
                for u in range(UNIT):
                    invs, delta = ready[u]
                    lows, dss = [], []
                    for f in range(BLOCK // CHUNK):
                        sub = pl.ds(c * BLOCK + f * CHUNK, CHUNK)
                        skip = f * CHUNK if c == i else 0
                        none = jnp.zeros((CHUNK, skip), jnp.bfloat16)
                        weight = scores[i % 2, u, sub, skip:] * invs[c * (BLOCK // CHUNK) + f][:, skip:]
                        change = weight * (gains[i % 2, u, sub, skip:] - delta[:, skip:])
                        lows.append(beside(none, weight.astype(jnp.bfloat16)))
                        dss.append(beside(none, change.astype(jnp.bfloat16)))
                    wide_low.append(jnp.concatenate(lows, axis=0))
                    ds = jnp.concatenate(dss, axis=0)
                    wide_ds.append(ds)
                    dqt[u] = dqt[u] + dot(kt[:, keys], ds, ((1,), (0,)))
                dv[keys] += dot(jnp.concatenate(wide_low, axis=1), gb, ((1,), (0,)))
                dk[keys] += dot(jnp.concatenate(wide_ds, axis=1), qb, ((1,), (0,)))
            for u in range(UNIT):
                keep_rows(dqs.at[u], i * BLOCK, spin(dqt[u].T * scale, at, -1.0).astype(jnp.bfloat16))

        ready = [start(u, 0) for u in range(UNIT)]
        for i in range(blocks):
            now = ready
            if i + 1 < blocks:
                ready = [start(u, i + 1) for u in range(UNIT)]
            finish(i, now)
        for u in range(UNIT):
            h = step * UNIT + u
            parcel = parcels.at[h]
            for b in range(spans):
                parcel[pl.ds(b * span, span)] = dqs[u, order[b]]
            column = pl.multiple_of((me * GROUP + EARLY + h) * HEAD_SIZE, HEAD_SIZE)
            scatter(parcel, dq_out.at[:, pl.ds(column, HEAD_SIZE)], 0)
        return carry

    lax.fori_loop(0, LATE // UNIT, group, 0)
    for copy in fetch(0):
        copy.wait()
    for b in range(spans):
        at = pl.ds(b * span, span)
        dqs[0, b] = spin(dk[at] * scale, at, -1.0).astype(jnp.bfloat16)
        dvs[b] = dv[at].astype(jnp.bfloat16)
    for b in range(spans):
        parcel_k[pl.ds(b * span, span)] = dqs[0, order[b]]
        parcel_v[pl.ds(b * span, span)] = dvs[order[b]]
    column = pl.ds(pl.multiple_of(me * HEAD_SIZE, HEAD_SIZE), HEAD_SIZE)
    scatter(parcel_k, dk_out.at[:, column], 1)
    scatter(parcel_v, dv_out.at[:, column], 2)
    away = HEAD_SIZE * (seq - 1)
    for sem in (send, recv):
        wait_bytes(dq_out.at[:, pl.ds(0, GROUP * away)], sem.at[0])
        wait_bytes(dk_out.at[:, pl.ds(0, away)], sem.at[1])
        wait_bytes(dv_out.at[:, pl.ds(0, away)], sem.at[2])
    wait_own(dq_out.at[:, pl.ds(0, GROUP * HEAD_SIZE)], own.at[0])
    wait_own(dk_out.at[:, pl.ds(0, HEAD_SIZE)], own.at[1])
    wait_own(dv_out.at[:, pl.ds(0, HEAD_SIZE)], own.at[2])


def attend(seq, order, inverse, table, q_late, g_late, ks, vs, dk, dv, early):
    tokens = ks.shape[0]
    rows = tokens // seq
    span = tokens // order.shape[0]
    smem = pl.BlockSpec(memory_space=pltpu.SMEM)
    vmem = pl.BlockSpec(memory_space=pltpu.VMEM)
    hbm = pl.BlockSpec(memory_space=pl.ANY)
    low = jnp.bfloat16
    thin = (tokens, HEAD_SIZE)
    tall = (tokens, BLOCK)
    return pl.pallas_call(
        functools.partial(attend_kernel, seq, span),
        out_shape=(
            jax.ShapeDtypeStruct((rows, seq * GROUP * HEAD_SIZE), low),
            jax.ShapeDtypeStruct((rows, seq * HEAD_SIZE), low),
            jax.ShapeDtypeStruct((rows, seq * HEAD_SIZE), low),
        ),
        in_specs=[smem, smem, hbm, vmem, vmem, hbm, vmem, vmem, vmem, hbm],
        out_specs=(hbm,) * 3,
        scratch_shapes=[
            pltpu.VMEM(thin, jnp.float32),
            pltpu.VMEM(thin, jnp.float32),
            pltpu.VMEM((UNIT,) + thin, low),
            pltpu.VMEM((UNIT,) + thin, low),
            pltpu.VMEM((HEAD_SIZE, tokens), low),
            pltpu.VMEM((tokens // span, span, HEAD_SIZE), low),
            pltpu.VMEM((tokens // span, span, HEAD_SIZE), low),
            pltpu.VMEM(thin, jnp.float32),
            pltpu.VMEM(thin, jnp.float32),
            pltpu.VMEM((2, UNIT) + tall, jnp.float32),
            pltpu.VMEM((2, UNIT) + tall, jnp.float32),
            pltpu.VMEM((UNIT, tokens // span, span, HEAD_SIZE), low),
            pltpu.VMEM((tokens // span, span, HEAD_SIZE), low),
            pltpu.VMEM((LATE,) + thin, low),
            pltpu.VMEM(thin, low),
            pltpu.VMEM(thin, low),
            pltpu.SemaphoreType.DMA((3,)),
            pltpu.SemaphoreType.DMA((3,)),
            pltpu.SemaphoreType.DMA((3,)),
            pltpu.SemaphoreType.DMA((2,)),
        ],
        compiler_params=pltpu.CompilerParams(
            collective_id=0, has_side_effects=True, vmem_limit_bytes=25 << 20
        ),
        name="attend",
    )(order, inverse, q_late, ks, vs, g_late, table, dk, dv, early)


def store_kernel(*refs):
    sources, targets, sem = refs[:3], refs[3:6], refs[6]
    copies = [
        pltpu.make_async_copy(source, target, sem.at[index])
        for index, (source, target) in enumerate(zip(sources, targets))
    ]
    for copy in copies:
        copy.start()
    for copy in copies:
        copy.wait()


def store(results):
    any_spec = pl.BlockSpec(memory_space=pl.ANY)
    return pl.pallas_call(
        store_kernel,
        out_shape=tuple(jax.ShapeDtypeStruct(a.shape, a.dtype) for a in results),
        in_specs=[any_spec] * 3,
        out_specs=(any_spec,) * 3,
        scratch_shapes=[pltpu.SemaphoreType.DMA((3,))],
        compiler_params=pltpu.CompilerParams(vmem_limit_bytes=2 << 20),
        name="store",
    )(*results)


def body(sections, seq, q, k, v, g, partner, order):
    span_index = jnp.arange(order.shape[0], dtype=jnp.int32)
    inverse = jnp.sum(
        jnp.where(order[:, None] == span_index[None, :], span_index[:, None], 0), axis=0
    )
    table = jnp.asarray(rotary_table(q.shape[2] * seq))
    span = q.shape[2] * seq // order.shape[0]
    parts = [a.reshape(-1, span, a.shape[-1]) for a in (q, k, v, g)]
    branches = [functools.partial(gather, pair, seq) for pair in range(1, sections)]
    moved = lax.switch(partner[0] - 1, branches, order, inverse, *parts, table)
    results = attend(seq, order, inverse, table, *moved)
    return tuple(result[None, None] for result in store(results))


def solution(mesh):
    placed = P("section", None, "seq", None)
    return jax.shard_map(
        functools.partial(body, mesh.shape["section"], mesh.shape["seq"]),
        mesh=mesh,
        in_specs=(placed, placed, placed, placed, P(), P()),
        out_specs=(placed, placed, placed),
        check_vma=False,
    )
```

```python
import functools
import math

import jax
import jax.numpy as jnp
import numpy as np
from jax import lax
from jax.experimental import pallas as pl
from jax.experimental.pallas import tpu as pltpu
from jax.sharding import PartitionSpec as P

QUERY_HEADS = 64
KEY_VALUE_HEADS = 8
HEAD_SIZE = 128
GROUP = QUERY_HEADS // KEY_VALUE_HEADS
BLOCK = 256
CHUNK = 128
UNIT = 1
EARLY = 2
LATE = GROUP - EARLY
MESH = pl.DeviceIdType.MESH
MIXED = ((1, 0), (3, 0), (0, 1), (2, 0), (1, 1), (3, 1), (2, 1), (0, 0))


def rotary_table(tokens):
    half = HEAD_SIZE // 2
    steps = np.arange(0, HEAD_SIZE, 2).astype(np.float32) / np.float32(HEAD_SIZE)
    frequency = np.power(np.float32(1000000.0), -steps).astype(np.float32)
    angles = np.arange(tokens, dtype=np.float32)[:, None] * frequency[None, :]
    angles = angles.astype(np.float64)
    table = np.concatenate([np.cos(angles), np.sin(angles)], axis=1).astype(np.float32)
    assert table.shape == (tokens, 2 * half)
    return table


def xor_static(index, mask):
    result = index
    bit = 1
    while bit <= mask:
        if mask & bit:
            low = lax.rem(lax.div(index, bit), 2)
            result = result + (1 - 2 * low) * bit
        bit *= 2
    return result


def wait_bytes(like, sem):
    pltpu.make_async_copy(like, like, sem).wait()


def wait_own(like, sem):
    pltpu.make_async_copy(like, like, sem).wait()


def peer(me, seq, dx, dz):
    lines = seq // 2
    return lax.rem(lax.div(me, 2) + dx, lines) * 2 + lax.rem(lax.rem(me, 2) + dz, 2)


def beside(left, right):
    return right if left.shape[1] == 0 else jnp.concatenate([left, right], axis=1)


def dot(a, b, dims):
    return lax.dot_general(a, b, (dims, ((), ())), preferred_element_type=jnp.float32)


def turn(work, x, at, sign):
    return x * work["cosine"][at] + sign * (pltpu.roll(x, HEAD_SIZE // 2, 1) * work["sine"][at])


def prepare_tables(work, table, span, spans):
    first = lax.broadcasted_iota(jnp.int32, (span, HEAD_SIZE), 1) < HEAD_SIZE // 2

    def step(b, carry):
        at = pl.ds(pl.multiple_of(b * span, span), span)
        both = table[at]
        swapped = pltpu.roll(both, HEAD_SIZE // 2, 1)
        work["cosine"][at] = jnp.where(first, both, swapped)
        work["sine"][at] = jnp.where(first, -swapped, both)
        return carry

    lax.fori_loop(0, spans, step, 0)


def invert(order, inverse, spans):
    def step(b, carry):
        found = jnp.int32(0)
        for j in range(spans):
            found = jnp.where(order[j] == b, jnp.int32(j), found)
        inverse[b] = found
        return carry

    lax.fori_loop(0, spans, step, 0)


def compact_head(work, span, spans, order, inverse, query_of, grad_of, parcel):
    qs, gs, ks, vs, kt = (work[name] for name in ("qs", "gs", "ks", "vs", "kt"))
    scores, gains, tops, dq = (work[name] for name in ("scores", "gains", "tops", "dq"))
    dk, dv, dqs = work["dk"], work["dv"], work["dqs"]
    scale = HEAD_SIZE**-0.5
    scale2 = scale * math.log2(math.e)
    parts = BLOCK // CHUNK
    rows = lax.broadcasted_iota(jnp.int32, (CHUNK, BLOCK), 0)
    lanes = lax.broadcasted_iota(jnp.int32, (CHUNK, BLOCK), 1)

    def sort(b, carry):
        at = pl.ds(pl.multiple_of(b * span, span), span)
        query = turn(work, query_of(inverse[b]).astype(jnp.float32), at, 1.0)
        qs[at] = query.astype(jnp.bfloat16)
        gs[at] = grad_of(inverse[b])
        return carry

    lax.fori_loop(0, spans, sort, 0)

    def block(i, carry):
        at = pl.ds(pl.multiple_of(i * BLOCK, BLOCK), BLOCK)

        def score(c, state, mask):
            top, total, mixed = state
            keys = pl.ds(pl.multiple_of(c * CHUNK, CHUNK), CHUNK)
            s = dot(ks[keys], qs[at], ((1,), (1,)))
            if mask is not None:
                s = jnp.where(rows + mask <= lanes, s, -jnp.inf)
            gain = dot(vs[keys], gs[at], ((1,), (1,)))
            new = jnp.max(jnp.max(s.reshape(CHUNK // 8, 8, BLOCK), axis=0), axis=0, keepdims=True)
            new = jnp.maximum(top, new)
            e = jnp.exp2((s - new) * scale2)
            scores[keys] = e
            gains[keys] = gain
            tops[c] = new
            fade = jnp.exp2((top - new) * scale2)
            total = total * fade + jnp.sum(e.reshape(CHUNK // 8, 8, BLOCK), axis=0)
            mixed = mixed * fade + jnp.sum((e * gain).reshape(CHUNK // 8, 8, BLOCK), axis=0)
            return new, total, mixed

        empty = jnp.zeros((8, BLOCK), jnp.float32)
        state = score(i * parts, (jnp.full((1, BLOCK), -jnp.inf), empty, empty), 0)
        for f in range(1, parts):
            state = score(i * parts + f, state, f * CHUNK)
        top, total, mixed = lax.fori_loop(
            0, i * parts, lambda c, now: score(c, now, None), state
        )
        inv = 1.0 / jnp.sum(total, axis=0, keepdims=True)
        delta = jnp.sum(mixed, axis=0, keepdims=True) * inv
        dq[...] = jnp.zeros_like(dq)

        def finish(c, carry):
            keys = pl.ds(pl.multiple_of(c * BLOCK, BLOCK), BLOCK)
            lows, dss = [], []
            for f in range(parts):
                sub = pl.ds(pl.multiple_of(c * BLOCK + f * CHUNK, CHUNK), CHUNK)
                factor = inv * jnp.exp2((tops[c * parts + f] - top) * scale2)
                weight = scores[sub] * factor
                lows.append(weight.astype(jnp.bfloat16))
                dss.append((weight * (gains[sub] - delta)).astype(jnp.bfloat16))
            low = jnp.concatenate(lows, axis=0)
            ds = jnp.concatenate(dss, axis=0)
            dv[keys] += dot(low, gs[at], ((1,), (0,)))
            dk[keys] += dot(ds, qs[at], ((1,), (0,)))
            dq[...] += dot(kt[:, keys], ds, ((1,), (0,)))
            return carry

        lax.fori_loop(0, i + 1, finish, 0)
        qs[at] = turn(work, dq[...].T * scale, at, -1.0).astype(jnp.bfloat16)
        return carry

    lax.fori_loop(0, spans * span // BLOCK, block, 0)

    def split(b, carry):
        dqs[b] = qs[pl.ds(pl.multiple_of(b * span, span), span)]
        return carry

    lax.fori_loop(0, spans, split, 0)

    def unsort(b, carry):
        parcel[pl.ds(pl.multiple_of(b * span, span), span)] = dqs[order[b]]
        return carry

    lax.fori_loop(0, spans, unsort, 0)


def gather_kernel(
    pair,
    seq,
    order,
    q_ref,
    k_ref,
    v_ref,
    g_ref,
    table_ref,
    q_late,
    g_late,
    ks_out,
    vs_out,
    dk_out,
    dv_out,
    early_out,
    inverse,
    ks,
    vs,
    dk,
    dv,
    parcels,
    q_early,
    g_early,
    k_land,
    v_land,
    table,
    cosine,
    sine,
    qs,
    gs,
    kt,
    scores,
    gains,
    tops,
    dq,
    dqs,
    send,
    recv,
    own,
):
    section = lax.axis_index("section")
    me = lax.axis_index("seq")
    other = xor_static(section, pair)
    held, span = q_ref.shape[:2]
    spans = held * seq
    targets = [(peer(me, seq, dx, dz), dx or dz) for dx, dz in MIXED]
    load = pltpu.make_async_copy(table_ref, table, own.at[2])
    load.start()
    barrier = pltpu.get_barrier_semaphore()
    for to, away in targets:
        pl.semaphore_signal(
            barrier, inc=1, device_id={"section": other, "seq": to}, device_id_type=MESH
        )
        if away:
            pl.semaphore_signal(
                barrier, inc=1, device_id={"section": section, "seq": to}, device_id_type=MESH
            )
    pl.semaphore_wait(barrier, 2 * seq - 1)
    mine = pl.ds(me * held, held)

    def column(block):
        return pl.ds(pl.multiple_of(block * HEAD_SIZE, HEAD_SIZE), HEAD_SIZE)

    def send_to(source, to, target, index, device):
        pltpu.make_async_remote_copy(
            src_ref=source,
            dst_ref=target,
            send_sem=send.at[index],
            recv_sem=recv.at[index],
            device_id={"section": device, "seq": to},
            device_id_type=MESH,
        ).start()

    def ship(first, count, q_target, g_target, index, local):
        def step(h, carry):
            for to, away in targets:
                wide = column(to * GROUP + first + h)
                send_to(q_ref.at[:, :, wide], to, q_target.at[h, mine], index, other)
                if away:
                    send_to(g_ref.at[:, :, wide], to, g_target.at[h, mine], index + 1, section)
            pltpu.make_async_copy(
                g_ref.at[:, :, column(me * GROUP + first + h)],
                g_target.at[h, mine],
                own.at[local],
            ).start()
            return carry

        lax.fori_loop(0, count, step, 0)

    for to, _ in targets:
        send_to(k_ref.at[:, :, column(to)], to, k_land.at[mine], 0, other)
        send_to(v_ref.at[:, :, column(to)], to, v_land.at[mine], 1, other)
    ship(0, EARLY, q_early, g_early, 2, 0)
    ship(EARLY, LATE, q_late, g_late, 4, 1)
    work = dict(
        cosine=cosine,
        sine=sine,
        qs=qs,
        gs=gs,
        ks=ks,
        vs=vs,
        kt=kt,
        scores=scores,
        gains=gains,
        tops=tops,
        dq=dq,
        dk=dk,
        dv=dv,
        dqs=dqs,
    )
    invert(order, inverse, spans)
    load.wait()
    prepare_tables(work, table, span, spans)
    dk[...] = jnp.zeros_like(dk)
    dv[...] = jnp.zeros_like(dv)
    others = pl.ds(0, spans - held)
    wait_bytes(k_land, recv.at[0])
    wait_bytes(v_land, recv.at[1])

    def place(b, carry):
        at = pl.ds(pl.multiple_of(b * span, span), span)
        key = turn(work, k_land[inverse[b]].astype(jnp.float32), at, 1.0)
        ks[at] = key.astype(jnp.bfloat16)
        vs[at] = v_land[inverse[b]]
        return carry

    lax.fori_loop(0, spans, place, 0)
    kt[...] = ks[...].T
    wait_bytes(q_early, recv.at[2])
    wait_bytes(g_early.at[:, others], recv.at[3])
    wait_own(g_early.at[:, pl.ds(0, held)], own.at[0])

    def head(h, carry):
        compact_head(
            work,
            span,
            spans,
            order,
            inverse,
            lambda b: q_early[h, b],
            lambda b: g_early[h, b],
            parcels.at[h],
        )
        return carry

    lax.fori_loop(0, EARLY, head, 0)
    results = [
        pltpu.make_async_copy(source, target, own.at[3 + index])
        for index, (source, target) in enumerate(
            ((ks, ks_out), (vs, vs_out), (dk, dk_out), (dv, dv_out), (parcels, early_out))
        )
    ]
    for copy in results:
        copy.start()
    wait_own(g_late.at[:, pl.ds(0, held)], own.at[1])
    wait_bytes(q_late, recv.at[4])
    wait_bytes(g_late.at[:, others], recv.at[5])
    wait_bytes(k_land, send.at[0])
    wait_bytes(v_land, send.at[1])
    wait_bytes(q_early, send.at[2])
    wait_bytes(g_early.at[:, others], send.at[3])
    wait_bytes(q_late, send.at[4])
    wait_bytes(g_late.at[:, others], send.at[5])
    for copy in results:
        copy.wait()


def gather(pair, seq, order, q, k, v, g, table):
    held, span = q.shape[:2]
    tokens = held * span * seq
    smem = pl.BlockSpec(memory_space=pltpu.SMEM)
    hbm = pl.BlockSpec(memory_space=pl.ANY)
    low = jnp.bfloat16
    thin = (tokens, HEAD_SIZE)
    blocks = (held * seq, span, HEAD_SIZE)
    late = jax.ShapeDtypeStruct((LATE,) + blocks, low)
    return pl.pallas_call(
        functools.partial(gather_kernel, pair, seq),
        out_shape=(
            late,
            late,
            jax.ShapeDtypeStruct(thin, low),
            jax.ShapeDtypeStruct(thin, low),
            jax.ShapeDtypeStruct(thin, jnp.float32),
            jax.ShapeDtypeStruct(thin, jnp.float32),
            jax.ShapeDtypeStruct((EARLY,) + thin, low),
        ),
        in_specs=[smem] + [hbm] * 5,
        out_specs=(hbm,) * 7,
        scratch_shapes=[
            pltpu.SMEM((held * seq,), jnp.int32),
            pltpu.VMEM(thin, low),
            pltpu.VMEM(thin, low),
            pltpu.VMEM(thin, jnp.float32),
            pltpu.VMEM(thin, jnp.float32),
            pltpu.VMEM((EARLY,) + thin, low),
            pltpu.VMEM((EARLY,) + blocks, low),
            pltpu.VMEM((EARLY,) + blocks, low),
            pltpu.VMEM(blocks, low),
            pltpu.VMEM(blocks, low),
            pltpu.VMEM(thin, jnp.float32),
            pltpu.VMEM(thin, jnp.float32),
            pltpu.VMEM(thin, jnp.float32),
            pltpu.VMEM(thin, low),
            pltpu.VMEM(thin, low),
            pltpu.VMEM((HEAD_SIZE, tokens), low),
            pltpu.VMEM((tokens, BLOCK), jnp.float32),
            pltpu.VMEM((tokens, BLOCK), jnp.float32),
            pltpu.VMEM((tokens // CHUNK, 1, BLOCK), jnp.float32),
            pltpu.VMEM((HEAD_SIZE, BLOCK), jnp.float32),
            pltpu.VMEM(blocks, low),
            pltpu.SemaphoreType.DMA((6,)),
            pltpu.SemaphoreType.DMA((6,)),
            pltpu.SemaphoreType.DMA((8,)),
        ],
        compiler_params=pltpu.CompilerParams(
            collective_id=pair, has_side_effects=True, vmem_limit_bytes=20 << 20
        ),
        name=f"gather_{pair}",
    )(order, q, k, v, g, table)


def attend_kernel(
    seq,
    span,
    order,
    q_all,
    ks_in,
    vs_in,
    g_all,
    table_in,
    dk_start,
    dv_start,
    early,
    dq_out,
    dk_out,
    dv_out,
    inverse,
    ks,
    vs,
    table,
    cosine,
    sine,
    qs,
    gs,
    kt,
    q_next,
    g_next,
    dk,
    dv,
    scores,
    gains,
    dqs,
    dvs,
    parcels,
    parcel_k,
    parcel_v,
    send,
    recv,
    own,
    load,
    fill,
):
    section = lax.axis_index("section")
    me = lax.axis_index("seq")
    tokens = ks_in.shape[0]
    spans = tokens // span
    rows = tokens // seq
    half = HEAD_SIZE // 2
    blocks = tokens // BLOCK
    scale = HEAD_SIZE**-0.5
    scale2 = scale * math.log2(math.e)
    filled = [
        pltpu.make_async_copy(source, target, fill.at[index])
        for index, (source, target) in enumerate(
            ((table_in, table), (ks_in, ks), (vs_in, vs), (dk_start, dk), (dv_start, dv))
        )
    ]
    for copy in filled:
        copy.start()
    barrier = pltpu.get_barrier_semaphore()
    for j in range(1, seq):
        pl.semaphore_signal(
            barrier,
            inc=1,
            device_id={"section": section, "seq": lax.rem(me + j, seq)},
            device_id_type=MESH,
        )
    pl.semaphore_wait(barrier, seq - 1)

    def fetch(h):
        return (
            pltpu.make_async_copy(q_all.at[h], q_next, load.at[0]),
            pltpu.make_async_copy(g_all.at[h], g_next, load.at[1]),
        )

    for copy in fetch(0):
        copy.start()

    def spin(x, at, sign):
        return x * cosine[at] + sign * (pltpu.roll(x, half, 1) * sine[at])

    diagonal = lax.broadcasted_iota(jnp.int32, (CHUNK, BLOCK), 0) <= lax.broadcasted_iota(
        jnp.int32, (CHUNK, BLOCK), 1
    )

    def send_to(source, target, index, to):
        pltpu.make_async_remote_copy(
            src_ref=source.at[pl.ds(pl.multiple_of(to * rows, rows), rows)],
            dst_ref=target,
            send_sem=send.at[index],
            recv_sem=recv.at[index],
            device_id={"section": section, "seq": to},
            device_id_type=MESH,
        ).start()

    def scatter(source, target, index):
        for dx, dz in MIXED:
            if dx or dz:
                send_to(source, target, index, peer(me, seq, dx, dz))
        pltpu.make_async_copy(
            source.at[pl.ds(pl.multiple_of(me * rows, rows), rows)], target, own.at[index]
        ).start()

    for h in range(EARLY):
        column = pl.multiple_of((me * GROUP + h) * HEAD_SIZE, HEAD_SIZE)
        scatter(early.at[h], dq_out.at[:, pl.ds(column, HEAD_SIZE)], 0)

    invert(order, inverse, spans)
    for copy in filled:
        copy.wait()
    prepare_tables({"cosine": cosine, "sine": sine}, table, span, spans)
    kt[...] = ks[...].T

    def keep_rows(target, start, value):
        stop = start + value.shape[0]
        row = start
        while row < stop:
            b, low = row // span, row % span
            size = min(span - low, stop - row)
            target[b, pl.ds(low, size)] = value[row - start : row - start + size]
            row += size

    def group(step, carry):
        for u in range(UNIT):
            h = step * UNIT + u
            for copy in fetch(h):
                copy.wait()
            for b in range(spans):
                at = pl.ds(b * span, span)
                query = spin(q_next[inverse[b]].astype(jnp.float32), at, 1.0)
                qs[u, at] = query.astype(jnp.bfloat16)
                gs[u, at] = g_next[inverse[b]]
            for copy in fetch(lax.rem(h + 1, LATE)):
                copy.start()

        def start(u, i):
            score, gain_keep = scores.at[i % 2, u], gains.at[i % 2, u]
            qb = qs[u, pl.ds(i * BLOCK, BLOCK)]
            gb = gs[u, pl.ds(i * BLOCK, BLOCK)]
            tops = []
            top = None
            for c in range((i + 1) * BLOCK // CHUNK):
                keys = pl.ds(c * CHUNK, CHUNK)
                skip = max(c * CHUNK - i * BLOCK, 0)
                width = BLOCK - skip
                s = dot(ks[keys], qb[skip:], ((1,), (1,)))
                if c * CHUNK >= i * BLOCK:
                    s = jnp.where(diagonal[:, :width], s, -jnp.inf)
                gain = dot(vs[keys], gb[skip:], ((1,), (1,)))
                new = jnp.max(jnp.max(s.reshape(CHUNK // 8, 8, width), axis=0), axis=0, keepdims=True)
                if top is not None:
                    new = jnp.maximum(top[:, skip:], new)
                e = jnp.exp2((s - new) * scale2)
                score[keys, skip:] = e
                gain_keep[keys, skip:] = gain
                tsum = jnp.sum(e.reshape(CHUNK // 8, 8, width), axis=0)
                msum = jnp.sum((e * gain).reshape(CHUNK // 8, 8, width), axis=0)
                if top is None:
                    total, mixed = tsum, msum
                else:
                    fade = jnp.exp2((top[:, skip:] - new) * scale2)
                    tsum = total[:, skip:] * fade + tsum
                    msum = mixed[:, skip:] * fade + msum
                    total = beside(total[:, :skip], tsum)
                    mixed = beside(mixed[:, :skip], msum)
                    new = beside(top[:, :skip], new)
                top = new
                tops.append(new)
            inv = 1.0 / jnp.sum(total, axis=0, keepdims=True)
            delta = jnp.sum(mixed, axis=0, keepdims=True) * inv
            return [inv * jnp.exp2((t - top) * scale2) for t in tops], delta

        def finish(i, ready):
            at = pl.ds(i * BLOCK, BLOCK)
            qb = jnp.concatenate([qs[u, at] for u in range(UNIT)], axis=0)
            gb = jnp.concatenate([gs[u, at] for u in range(UNIT)], axis=0)
            dqt = [jnp.zeros((HEAD_SIZE, BLOCK), jnp.float32)] * UNIT
            for c in range(i + 1):
                keys = pl.ds(c * BLOCK, BLOCK)
                wide_low, wide_ds = [], []
                for u in range(UNIT):
                    invs, delta = ready[u]
                    lows, dss = [], []
                    for f in range(BLOCK // CHUNK):
                        sub = pl.ds(c * BLOCK + f * CHUNK, CHUNK)
                        skip = f * CHUNK if c == i else 0
                        none = jnp.zeros((CHUNK, skip), jnp.bfloat16)
                        weight = scores[i % 2, u, sub, skip:] * invs[c * (BLOCK // CHUNK) + f][:, skip:]
                        change = weight * (gains[i % 2, u, sub, skip:] - delta[:, skip:])
                        lows.append(beside(none, weight.astype(jnp.bfloat16)))
                        dss.append(beside(none, change.astype(jnp.bfloat16)))
                    wide_low.append(jnp.concatenate(lows, axis=0))
                    ds = jnp.concatenate(dss, axis=0)
                    wide_ds.append(ds)
                    dqt[u] = dqt[u] + dot(kt[:, keys], ds, ((1,), (0,)))
                dv[keys] += dot(jnp.concatenate(wide_low, axis=1), gb, ((1,), (0,)))
                dk[keys] += dot(jnp.concatenate(wide_ds, axis=1), qb, ((1,), (0,)))
            for u in range(UNIT):
                keep_rows(dqs.at[u], i * BLOCK, spin(dqt[u].T * scale, at, -1.0).astype(jnp.bfloat16))

        ready = [start(u, 0) for u in range(UNIT)]
        for i in range(blocks):
            now = ready
            if i + 1 < blocks:
                ready = [start(u, i + 1) for u in range(UNIT)]
            finish(i, now)
        for u in range(UNIT):
            h = step * UNIT + u
            parcel = parcels.at[h]
            for b in range(spans):
                parcel[pl.ds(b * span, span)] = dqs[u, order[b]]
            column = pl.multiple_of((me * GROUP + EARLY + h) * HEAD_SIZE, HEAD_SIZE)
            scatter(parcel, dq_out.at[:, pl.ds(column, HEAD_SIZE)], 0)
        return carry

    lax.fori_loop(0, LATE // UNIT, group, 0)
    for copy in fetch(0):
        copy.wait()
    for b in range(spans):
        at = pl.ds(b * span, span)
        dqs[0, b] = spin(dk[at] * scale, at, -1.0).astype(jnp.bfloat16)
        dvs[b] = dv[at].astype(jnp.bfloat16)
    for b in range(spans):
        parcel_k[pl.ds(b * span, span)] = dqs[0, order[b]]
        parcel_v[pl.ds(b * span, span)] = dvs[order[b]]
    column = pl.ds(pl.multiple_of(me * HEAD_SIZE, HEAD_SIZE), HEAD_SIZE)
    scatter(parcel_k, dk_out.at[:, column], 1)
    scatter(parcel_v, dv_out.at[:, column], 2)
    away = HEAD_SIZE * (seq - 1)
    for sem in (send, recv):
        wait_bytes(dq_out.at[:, pl.ds(0, GROUP * away)], sem.at[0])
        wait_bytes(dk_out.at[:, pl.ds(0, away)], sem.at[1])
        wait_bytes(dv_out.at[:, pl.ds(0, away)], sem.at[2])
    wait_own(dq_out.at[:, pl.ds(0, GROUP * HEAD_SIZE)], own.at[0])
    wait_own(dk_out.at[:, pl.ds(0, HEAD_SIZE)], own.at[1])
    wait_own(dv_out.at[:, pl.ds(0, HEAD_SIZE)], own.at[2])


def attend(seq, order, table, q_late, g_late, ks, vs, dk, dv, early):
    tokens = ks.shape[0]
    rows = tokens // seq
    span = tokens // order.shape[0]
    smem = pl.BlockSpec(memory_space=pltpu.SMEM)
    hbm = pl.BlockSpec(memory_space=pl.ANY)
    low = jnp.bfloat16
    thin = (tokens, HEAD_SIZE)
    tall = (tokens, BLOCK)
    return pl.pallas_call(
        functools.partial(attend_kernel, seq, span),
        out_shape=(
            jax.ShapeDtypeStruct((rows, seq * GROUP * HEAD_SIZE), low),
            jax.ShapeDtypeStruct((rows, seq * HEAD_SIZE), low),
            jax.ShapeDtypeStruct((rows, seq * HEAD_SIZE), low),
        ),
        in_specs=[smem] + [hbm] * 8,
        out_specs=(hbm,) * 3,
        scratch_shapes=[
            pltpu.SMEM((tokens // span,), jnp.int32),
            pltpu.VMEM(thin, low),
            pltpu.VMEM(thin, low),
            pltpu.VMEM(thin, jnp.float32),
            pltpu.VMEM(thin, jnp.float32),
            pltpu.VMEM(thin, jnp.float32),
            pltpu.VMEM((UNIT,) + thin, low),
            pltpu.VMEM((UNIT,) + thin, low),
            pltpu.VMEM((HEAD_SIZE, tokens), low),
            pltpu.VMEM((tokens // span, span, HEAD_SIZE), low),
            pltpu.VMEM((tokens // span, span, HEAD_SIZE), low),
            pltpu.VMEM(thin, jnp.float32),
            pltpu.VMEM(thin, jnp.float32),
            pltpu.VMEM((2, UNIT) + tall, jnp.float32),
            pltpu.VMEM((2, UNIT) + tall, jnp.float32),
            pltpu.VMEM((UNIT, tokens // span, span, HEAD_SIZE), low),
            pltpu.VMEM((tokens // span, span, HEAD_SIZE), low),
            pltpu.VMEM((LATE,) + thin, low),
            pltpu.VMEM(thin, low),
            pltpu.VMEM(thin, low),
            pltpu.SemaphoreType.DMA((3,)),
            pltpu.SemaphoreType.DMA((3,)),
            pltpu.SemaphoreType.DMA((3,)),
            pltpu.SemaphoreType.DMA((2,)),
            pltpu.SemaphoreType.DMA((5,)),
        ],
        compiler_params=pltpu.CompilerParams(
            collective_id=0, has_side_effects=True, vmem_limit_bytes=25 << 20
        ),
        name="attend",
    )(order, q_late, ks, vs, g_late, table, dk, dv, early)


def store_kernel(*refs):
    sources, targets, sem = refs[:3], refs[3:6], refs[6]
    copies = [
        pltpu.make_async_copy(source, target, sem.at[index])
        for index, (source, target) in enumerate(zip(sources, targets))
    ]
    for copy in copies:
        copy.start()
    for copy in copies:
        copy.wait()


def store(results):
    any_spec = pl.BlockSpec(memory_space=pl.ANY)
    return pl.pallas_call(
        store_kernel,
        out_shape=tuple(jax.ShapeDtypeStruct(a.shape, a.dtype) for a in results),
        in_specs=[any_spec] * 3,
        out_specs=(any_spec,) * 3,
        scratch_shapes=[pltpu.SemaphoreType.DMA((3,))],
        compiler_params=pltpu.CompilerParams(vmem_limit_bytes=2 << 20),
        name="store",
    )(*results)


def body(sections, seq, q, k, v, g, partner, order):
    table = jnp.asarray(rotary_table(q.shape[2] * seq))
    span = q.shape[2] * seq // order.shape[0]
    parts = [a.reshape(-1, span, a.shape[-1]) for a in (q, k, v, g)]
    branches = [functools.partial(gather, pair, seq) for pair in range(1, sections)]
    moved = lax.switch(partner[0] - 1, branches, order, *parts, table)
    results = attend(seq, order, table, *moved)
    return tuple(result[None, None] for result in store(results))


def solution(mesh):
    placed = P("section", None, "seq", None)
    return jax.shard_map(
        functools.partial(body, mesh.shape["section"], mesh.shape["seq"]),
        mesh=mesh,
        in_specs=(placed, placed, placed, placed, P(), P()),
        out_specs=(placed, placed, placed),
        check_vma=False,
    )
```

```python
import functools
import math

import jax
import jax.numpy as jnp
import numpy as np
from jax import lax
from jax.experimental import pallas as pl
from jax.experimental.pallas import tpu as pltpu
from jax.sharding import PartitionSpec as P

QUERY_HEADS = 64
KEY_VALUE_HEADS = 8
HEAD_SIZE = 128
GROUP = QUERY_HEADS // KEY_VALUE_HEADS
BLOCK = 256
CHUNK = 128
UNIT = 1
EARLY = 1
LATE = GROUP - EARLY
MESH = pl.DeviceIdType.MESH
MIXED = ((1, 0), (3, 0), (0, 1), (2, 0), (1, 1), (3, 1), (2, 1), (0, 0))


def rotary_table(tokens):
    half = HEAD_SIZE // 2
    steps = np.arange(0, HEAD_SIZE, 2).astype(np.float32) / np.float32(HEAD_SIZE)
    frequency = np.power(np.float32(1000000.0), -steps).astype(np.float32)
    angles = np.arange(tokens, dtype=np.float32)[:, None] * frequency[None, :]
    angles = angles.astype(np.float64)
    table = np.concatenate([np.cos(angles), np.sin(angles)], axis=1).astype(np.float32)
    assert table.shape == (tokens, 2 * half)
    return table


def xor_static(index, mask):
    result = index
    bit = 1
    while bit <= mask:
        if mask & bit:
            low = lax.rem(lax.div(index, bit), 2)
            result = result + (1 - 2 * low) * bit
        bit *= 2
    return result


def wait_bytes(like, sem):
    pltpu.make_async_copy(like, like, sem).wait()


def wait_own(like, sem):
    pltpu.make_async_copy(like, like, sem).wait()


def peer(me, seq, dx, dz):
    lines = seq // 2
    return lax.rem(lax.div(me, 2) + dx, lines) * 2 + lax.rem(lax.rem(me, 2) + dz, 2)


def beside(left, right):
    return right if left.shape[1] == 0 else jnp.concatenate([left, right], axis=1)


def dot(a, b, dims):
    return lax.dot_general(a, b, (dims, ((), ())), preferred_element_type=jnp.float32)


def turn(work, x, at, sign):
    return x * work["cosine"][at] + sign * (pltpu.roll(x, HEAD_SIZE // 2, 1) * work["sine"][at])


def prepare_tables(work, table, span, spans):
    first = lax.broadcasted_iota(jnp.int32, (span, HEAD_SIZE), 1) < HEAD_SIZE // 2

    def step(b, carry):
        at = pl.ds(pl.multiple_of(b * span, span), span)
        both = table[at]
        swapped = pltpu.roll(both, HEAD_SIZE // 2, 1)
        work["cosine"][at] = jnp.where(first, both, swapped)
        work["sine"][at] = jnp.where(first, -swapped, both)
        return carry

    lax.fori_loop(0, spans, step, 0)


def invert(order, inverse, spans):
    def step(b, carry):
        found = jnp.int32(0)
        for j in range(spans):
            found = jnp.where(order[j] == b, jnp.int32(j), found)
        inverse[b] = found
        return carry

    lax.fori_loop(0, spans, step, 0)


def compact_head(work, span, spans, order, inverse, query_of, grad_of, parcel):
    qs, gs, ks, vs, kt = (work[name] for name in ("qs", "gs", "ks", "vs", "kt"))
    scores, gains, tops, dq = (work[name] for name in ("scores", "gains", "tops", "dq"))
    dk, dv, dqs = work["dk"], work["dv"], work["dqs"]
    scale = HEAD_SIZE**-0.5
    scale2 = scale * math.log2(math.e)
    parts = BLOCK // CHUNK
    rows = lax.broadcasted_iota(jnp.int32, (CHUNK, BLOCK), 0)
    lanes = lax.broadcasted_iota(jnp.int32, (CHUNK, BLOCK), 1)

    def sort(b, carry):
        at = pl.ds(pl.multiple_of(b * span, span), span)
        query = turn(work, query_of(inverse[b]).astype(jnp.float32), at, 1.0)
        qs[at] = query.astype(jnp.bfloat16)
        gs[at] = grad_of(inverse[b])
        return carry

    lax.fori_loop(0, spans, sort, 0)

    def block(i, carry):
        at = pl.ds(pl.multiple_of(i * BLOCK, BLOCK), BLOCK)

        def score(c, state, mask):
            top, total, mixed = state
            keys = pl.ds(pl.multiple_of(c * CHUNK, CHUNK), CHUNK)
            s = dot(ks[keys], qs[at], ((1,), (1,)))
            if mask is not None:
                s = jnp.where(rows + mask <= lanes, s, -jnp.inf)
            gain = dot(vs[keys], gs[at], ((1,), (1,)))
            new = jnp.max(jnp.max(s.reshape(CHUNK // 8, 8, BLOCK), axis=0), axis=0, keepdims=True)
            new = jnp.maximum(top, new)
            e = jnp.exp2((s - new) * scale2)
            scores[keys] = e
            gains[keys] = gain
            tops[c] = new
            fade = jnp.exp2((top - new) * scale2)
            total = total * fade + jnp.sum(e.reshape(CHUNK // 8, 8, BLOCK), axis=0)
            mixed = mixed * fade + jnp.sum((e * gain).reshape(CHUNK // 8, 8, BLOCK), axis=0)
            return new, total, mixed

        empty = jnp.zeros((8, BLOCK), jnp.float32)
        state = score(i * parts, (jnp.full((1, BLOCK), -jnp.inf), empty, empty), 0)
        for f in range(1, parts):
            state = score(i * parts + f, state, f * CHUNK)
        top, total, mixed = lax.fori_loop(
            0, i * parts, lambda c, now: score(c, now, None), state
        )
        inv = 1.0 / jnp.sum(total, axis=0, keepdims=True)
        delta = jnp.sum(mixed, axis=0, keepdims=True) * inv
        dq[...] = jnp.zeros_like(dq)

        def finish(c, carry):
            keys = pl.ds(pl.multiple_of(c * BLOCK, BLOCK), BLOCK)
            lows, dss = [], []
            for f in range(parts):
                sub = pl.ds(pl.multiple_of(c * BLOCK + f * CHUNK, CHUNK), CHUNK)
                factor = inv * jnp.exp2((tops[c * parts + f] - top) * scale2)
                weight = scores[sub] * factor
                lows.append(weight.astype(jnp.bfloat16))
                dss.append((weight * (gains[sub] - delta)).astype(jnp.bfloat16))
            low = jnp.concatenate(lows, axis=0)
            ds = jnp.concatenate(dss, axis=0)
            dv[keys] += dot(low, gs[at], ((1,), (0,)))
            dk[keys] += dot(ds, qs[at], ((1,), (0,)))
            dq[...] += dot(kt[:, keys], ds, ((1,), (0,)))
            return carry

        lax.fori_loop(0, i + 1, finish, 0)
        qs[at] = turn(work, dq[...].T * scale, at, -1.0).astype(jnp.bfloat16)
        return carry

    lax.fori_loop(0, spans * span // BLOCK, block, 0)

    def split(b, carry):
        dqs[b] = qs[pl.ds(pl.multiple_of(b * span, span), span)]
        return carry

    lax.fori_loop(0, spans, split, 0)

    def unsort(b, carry):
        parcel[pl.ds(pl.multiple_of(b * span, span), span)] = dqs[order[b]]
        return carry

    lax.fori_loop(0, spans, unsort, 0)


def gather_kernel(
    pair,
    seq,
    order,
    q_ref,
    k_ref,
    v_ref,
    g_ref,
    table_ref,
    q_late,
    g_late,
    ks_out,
    vs_out,
    dk_out,
    dv_out,
    early_out,
    inverse,
    ks,
    vs,
    dk,
    dv,
    parcels,
    q_early,
    g_early,
    k_land,
    v_land,
    table,
    cosine,
    sine,
    qs,
    gs,
    kt,
    scores,
    gains,
    tops,
    dq,
    dqs,
    send,
    recv,
    own,
):
    section = lax.axis_index("section")
    me = lax.axis_index("seq")
    other = xor_static(section, pair)
    held, span = q_ref.shape[:2]
    spans = held * seq
    targets = [(peer(me, seq, dx, dz), dx or dz) for dx, dz in MIXED]
    load = pltpu.make_async_copy(table_ref, table, own.at[2])
    load.start()
    barrier = pltpu.get_barrier_semaphore()
    for to, away in targets:
        pl.semaphore_signal(
            barrier, inc=1, device_id={"section": other, "seq": to}, device_id_type=MESH
        )
        if away:
            pl.semaphore_signal(
                barrier, inc=1, device_id={"section": section, "seq": to}, device_id_type=MESH
            )
    pl.semaphore_wait(barrier, 2 * seq - 1)
    mine = pl.ds(me * held, held)

    def column(block):
        return pl.ds(pl.multiple_of(block * HEAD_SIZE, HEAD_SIZE), HEAD_SIZE)

    def send_to(source, to, target, index, device):
        pltpu.make_async_remote_copy(
            src_ref=source,
            dst_ref=target,
            send_sem=send.at[index],
            recv_sem=recv.at[index],
            device_id={"section": device, "seq": to},
            device_id_type=MESH,
        ).start()

    def ship(first, count, q_target, g_target, index, local):
        def step(h, carry):
            for to, away in targets:
                wide = column(to * GROUP + first + h)
                send_to(q_ref.at[:, :, wide], to, q_target.at[h, mine], index, other)
                if away:
                    send_to(g_ref.at[:, :, wide], to, g_target.at[h, mine], index + 1, section)
            pltpu.make_async_copy(
                g_ref.at[:, :, column(me * GROUP + first + h)],
                g_target.at[h, mine],
                own.at[local],
            ).start()
            return carry

        lax.fori_loop(0, count, step, 0)

    for to, _ in targets:
        send_to(k_ref.at[:, :, column(to)], to, k_land.at[mine], 0, other)
        send_to(v_ref.at[:, :, column(to)], to, v_land.at[mine], 1, other)
    ship(0, EARLY, q_early, g_early, 2, 0)
    ship(EARLY, LATE, q_late, g_late, 4, 1)
    work = dict(
        cosine=cosine,
        sine=sine,
        qs=qs,
        gs=gs,
        ks=ks,
        vs=vs,
        kt=kt,
        scores=scores,
        gains=gains,
        tops=tops,
        dq=dq,
        dk=dk,
        dv=dv,
        dqs=dqs,
    )
    invert(order, inverse, spans)
    load.wait()
    prepare_tables(work, table, span, spans)
    dk[...] = jnp.zeros_like(dk)
    dv[...] = jnp.zeros_like(dv)
    others = pl.ds(0, spans - held)
    wait_bytes(k_land, recv.at[0])
    wait_bytes(v_land, recv.at[1])

    def place(b, carry):
        at = pl.ds(pl.multiple_of(b * span, span), span)
        key = turn(work, k_land[inverse[b]].astype(jnp.float32), at, 1.0)
        ks[at] = key.astype(jnp.bfloat16)
        vs[at] = v_land[inverse[b]]
        return carry

    lax.fori_loop(0, spans, place, 0)
    kt[...] = ks[...].T
    wait_bytes(q_early, recv.at[2])
    wait_bytes(g_early.at[:, others], recv.at[3])
    wait_own(g_early.at[:, pl.ds(0, held)], own.at[0])

    def head(h, carry):
        compact_head(
            work,
            span,
            spans,
            order,
            inverse,
            lambda b: q_early[h, b],
            lambda b: g_early[h, b],
            parcels.at[h],
        )
        return carry

    lax.fori_loop(0, EARLY, head, 0)
    results = [
        pltpu.make_async_copy(source, target, own.at[3 + index])
        for index, (source, target) in enumerate(
            ((ks, ks_out), (vs, vs_out), (dk, dk_out), (dv, dv_out), (parcels, early_out))
        )
    ]
    for copy in results:
        copy.start()
    wait_own(g_late.at[:, pl.ds(0, held)], own.at[1])
    wait_bytes(q_late, recv.at[4])
    wait_bytes(g_late.at[:, others], recv.at[5])
    wait_bytes(k_land, send.at[0])
    wait_bytes(v_land, send.at[1])
    wait_bytes(q_early, send.at[2])
    wait_bytes(g_early.at[:, others], send.at[3])
    wait_bytes(q_late, send.at[4])
    wait_bytes(g_late.at[:, others], send.at[5])
    for copy in results:
        copy.wait()


def gather(pair, seq, order, q, k, v, g, table):
    held, span = q.shape[:2]
    tokens = held * span * seq
    smem = pl.BlockSpec(memory_space=pltpu.SMEM)
    hbm = pl.BlockSpec(memory_space=pl.ANY)
    low = jnp.bfloat16
    thin = (tokens, HEAD_SIZE)
    blocks = (held * seq, span, HEAD_SIZE)
    late = jax.ShapeDtypeStruct((LATE,) + blocks, low)
    return pl.pallas_call(
        functools.partial(gather_kernel, pair, seq),
        out_shape=(
            late,
            late,
            jax.ShapeDtypeStruct(thin, low),
            jax.ShapeDtypeStruct(thin, low),
            jax.ShapeDtypeStruct(thin, jnp.float32),
            jax.ShapeDtypeStruct(thin, jnp.float32),
            jax.ShapeDtypeStruct((EARLY,) + thin, low),
        ),
        in_specs=[smem] + [hbm] * 5,
        out_specs=(hbm,) * 7,
        scratch_shapes=[
            pltpu.SMEM((held * seq,), jnp.int32),
            pltpu.VMEM(thin, low),
            pltpu.VMEM(thin, low),
            pltpu.VMEM(thin, jnp.float32),
            pltpu.VMEM(thin, jnp.float32),
            pltpu.VMEM((EARLY,) + thin, low),
            pltpu.VMEM((EARLY,) + blocks, low),
            pltpu.VMEM((EARLY,) + blocks, low),
            pltpu.VMEM(blocks, low),
            pltpu.VMEM(blocks, low),
            pltpu.VMEM(thin, jnp.float32),
            pltpu.VMEM(thin, jnp.float32),
            pltpu.VMEM(thin, jnp.float32),
            pltpu.VMEM(thin, low),
            pltpu.VMEM(thin, low),
            pltpu.VMEM((HEAD_SIZE, tokens), low),
            pltpu.VMEM((tokens, BLOCK), jnp.float32),
            pltpu.VMEM((tokens, BLOCK), jnp.float32),
            pltpu.VMEM((tokens // CHUNK, 1, BLOCK), jnp.float32),
            pltpu.VMEM((HEAD_SIZE, BLOCK), jnp.float32),
            pltpu.VMEM(blocks, low),
            pltpu.SemaphoreType.DMA((6,)),
            pltpu.SemaphoreType.DMA((6,)),
            pltpu.SemaphoreType.DMA((8,)),
        ],
        compiler_params=pltpu.CompilerParams(
            collective_id=pair, has_side_effects=True, vmem_limit_bytes=20 << 20
        ),
        name=f"gather_{pair}",
    )(order, q, k, v, g, table)


def attend_kernel(
    seq,
    span,
    order,
    q_all,
    ks_in,
    vs_in,
    g_all,
    table_in,
    dk_start,
    dv_start,
    early,
    dq_out,
    dk_out,
    dv_out,
    inverse,
    ks,
    vs,
    table,
    cosine,
    sine,
    qs,
    gs,
    kt,
    q_next,
    g_next,
    dk,
    dv,
    scores,
    gains,
    dqs,
    dvs,
    parcels,
    parcel_k,
    parcel_v,
    send,
    recv,
    own,
    load,
    fill,
):
    section = lax.axis_index("section")
    me = lax.axis_index("seq")
    tokens = ks_in.shape[0]
    spans = tokens // span
    rows = tokens // seq
    half = HEAD_SIZE // 2
    blocks = tokens // BLOCK
    scale = HEAD_SIZE**-0.5
    scale2 = scale * math.log2(math.e)
    filled = [
        pltpu.make_async_copy(source, target, fill.at[index])
        for index, (source, target) in enumerate(
            ((table_in, table), (ks_in, ks), (vs_in, vs), (dk_start, dk), (dv_start, dv))
        )
    ]
    for copy in filled:
        copy.start()
    barrier = pltpu.get_barrier_semaphore()
    for j in range(1, seq):
        pl.semaphore_signal(
            barrier,
            inc=1,
            device_id={"section": section, "seq": lax.rem(me + j, seq)},
            device_id_type=MESH,
        )
    pl.semaphore_wait(barrier, seq - 1)

    def fetch(h):
        return (
            pltpu.make_async_copy(q_all.at[h], q_next, load.at[0]),
            pltpu.make_async_copy(g_all.at[h], g_next, load.at[1]),
        )

    for copy in fetch(0):
        copy.start()

    def spin(x, at, sign):
        return x * cosine[at] + sign * (pltpu.roll(x, half, 1) * sine[at])

    diagonal = lax.broadcasted_iota(jnp.int32, (CHUNK, BLOCK), 0) <= lax.broadcasted_iota(
        jnp.int32, (CHUNK, BLOCK), 1
    )

    def send_to(source, target, index, to):
        pltpu.make_async_remote_copy(
            src_ref=source.at[pl.ds(pl.multiple_of(to * rows, rows), rows)],
            dst_ref=target,
            send_sem=send.at[index],
            recv_sem=recv.at[index],
            device_id={"section": section, "seq": to},
            device_id_type=MESH,
        ).start()

    def scatter(source, target, index):
        for dx, dz in MIXED:
            if dx or dz:
                send_to(source, target, index, peer(me, seq, dx, dz))
        pltpu.make_async_copy(
            source.at[pl.ds(pl.multiple_of(me * rows, rows), rows)], target, own.at[index]
        ).start()

    for h in range(EARLY):
        column = pl.multiple_of((me * GROUP + h) * HEAD_SIZE, HEAD_SIZE)
        scatter(early.at[h], dq_out.at[:, pl.ds(column, HEAD_SIZE)], 0)

    invert(order, inverse, spans)
    for copy in filled:
        copy.wait()
    prepare_tables({"cosine": cosine, "sine": sine}, table, span, spans)
    kt[...] = ks[...].T

    def keep_rows(target, start, value):
        stop = start + value.shape[0]
        row = start
        while row < stop:
            b, low = row // span, row % span
            size = min(span - low, stop - row)
            target[b, pl.ds(low, size)] = value[row - start : row - start + size]
            row += size

    def group(step, carry):
        for u in range(UNIT):
            h = step * UNIT + u
            for copy in fetch(h):
                copy.wait()
            for b in range(spans):
                at = pl.ds(b * span, span)
                query = spin(q_next[inverse[b]].astype(jnp.float32), at, 1.0)
                qs[u, at] = query.astype(jnp.bfloat16)
                gs[u, at] = g_next[inverse[b]]
            for copy in fetch(lax.rem(h + 1, LATE)):
                copy.start()

        def start(u, i):
            score, gain_keep = scores.at[i % 2, u], gains.at[i % 2, u]
            qb = qs[u, pl.ds(i * BLOCK, BLOCK)]
            gb = gs[u, pl.ds(i * BLOCK, BLOCK)]
            tops = []
            top = None
            for c in range((i + 1) * BLOCK // CHUNK):
                keys = pl.ds(c * CHUNK, CHUNK)
                skip = max(c * CHUNK - i * BLOCK, 0)
                width = BLOCK - skip
                s = dot(ks[keys], qb[skip:], ((1,), (1,)))
                if c * CHUNK >= i * BLOCK:
                    s = jnp.where(diagonal[:, :width], s, -jnp.inf)
                gain = dot(vs[keys], gb[skip:], ((1,), (1,)))
                new = jnp.max(jnp.max(s.reshape(CHUNK // 8, 8, width), axis=0), axis=0, keepdims=True)
                if top is not None:
                    new = jnp.maximum(top[:, skip:], new)
                e = jnp.exp2((s - new) * scale2)
                score[keys, skip:] = e
                gain_keep[keys, skip:] = gain
                tsum = jnp.sum(e.reshape(CHUNK // 8, 8, width), axis=0)
                msum = jnp.sum((e * gain).reshape(CHUNK // 8, 8, width), axis=0)
                if top is None:
                    total, mixed = tsum, msum
                else:
                    fade = jnp.exp2((top[:, skip:] - new) * scale2)
                    tsum = total[:, skip:] * fade + tsum
                    msum = mixed[:, skip:] * fade + msum
                    total = beside(total[:, :skip], tsum)
                    mixed = beside(mixed[:, :skip], msum)
                    new = beside(top[:, :skip], new)
                top = new
                tops.append(new)
            inv = 1.0 / jnp.sum(total, axis=0, keepdims=True)
            delta = jnp.sum(mixed, axis=0, keepdims=True) * inv
            return [inv * jnp.exp2((t - top) * scale2) for t in tops], delta

        def finish(i, ready):
            at = pl.ds(i * BLOCK, BLOCK)
            qb = jnp.concatenate([qs[u, at] for u in range(UNIT)], axis=0)
            gb = jnp.concatenate([gs[u, at] for u in range(UNIT)], axis=0)
            dqt = [jnp.zeros((HEAD_SIZE, BLOCK), jnp.float32)] * UNIT
            for c in range(i + 1):
                keys = pl.ds(c * BLOCK, BLOCK)
                wide_low, wide_ds = [], []
                for u in range(UNIT):
                    invs, delta = ready[u]
                    lows, dss = [], []
                    for f in range(BLOCK // CHUNK):
                        sub = pl.ds(c * BLOCK + f * CHUNK, CHUNK)
                        skip = f * CHUNK if c == i else 0
                        none = jnp.zeros((CHUNK, skip), jnp.bfloat16)
                        weight = scores[i % 2, u, sub, skip:] * invs[c * (BLOCK // CHUNK) + f][:, skip:]
                        change = weight * (gains[i % 2, u, sub, skip:] - delta[:, skip:])
                        lows.append(beside(none, weight.astype(jnp.bfloat16)))
                        dss.append(beside(none, change.astype(jnp.bfloat16)))
                    wide_low.append(jnp.concatenate(lows, axis=0))
                    ds = jnp.concatenate(dss, axis=0)
                    wide_ds.append(ds)
                    dqt[u] = dqt[u] + dot(kt[:, keys], ds, ((1,), (0,)))
                dv[keys] += dot(jnp.concatenate(wide_low, axis=1), gb, ((1,), (0,)))
                dk[keys] += dot(jnp.concatenate(wide_ds, axis=1), qb, ((1,), (0,)))
            for u in range(UNIT):
                keep_rows(dqs.at[u], i * BLOCK, spin(dqt[u].T * scale, at, -1.0).astype(jnp.bfloat16))

        ready = [start(u, 0) for u in range(UNIT)]
        for i in range(blocks):
            now = ready
            if i + 1 < blocks:
                ready = [start(u, i + 1) for u in range(UNIT)]
            finish(i, now)
        for u in range(UNIT):
            h = step * UNIT + u
            parcel = parcels.at[h]
            for b in range(spans):
                parcel[pl.ds(b * span, span)] = dqs[u, order[b]]
            column = pl.multiple_of((me * GROUP + EARLY + h) * HEAD_SIZE, HEAD_SIZE)
            scatter(parcel, dq_out.at[:, pl.ds(column, HEAD_SIZE)], 0)
        return carry

    lax.fori_loop(0, LATE // UNIT, group, 0)
    for copy in fetch(0):
        copy.wait()
    for b in range(spans):
        at = pl.ds(b * span, span)
        dqs[0, b] = spin(dk[at] * scale, at, -1.0).astype(jnp.bfloat16)
        dvs[b] = dv[at].astype(jnp.bfloat16)
    for b in range(spans):
        parcel_k[pl.ds(b * span, span)] = dqs[0, order[b]]
        parcel_v[pl.ds(b * span, span)] = dvs[order[b]]
    column = pl.ds(pl.multiple_of(me * HEAD_SIZE, HEAD_SIZE), HEAD_SIZE)
    scatter(parcel_k, dk_out.at[:, column], 1)
    scatter(parcel_v, dv_out.at[:, column], 2)
    away = HEAD_SIZE * (seq - 1)
    for sem in (send, recv):
        wait_bytes(dq_out.at[:, pl.ds(0, GROUP * away)], sem.at[0])
        wait_bytes(dk_out.at[:, pl.ds(0, away)], sem.at[1])
        wait_bytes(dv_out.at[:, pl.ds(0, away)], sem.at[2])
    wait_own(dq_out.at[:, pl.ds(0, GROUP * HEAD_SIZE)], own.at[0])
    wait_own(dk_out.at[:, pl.ds(0, HEAD_SIZE)], own.at[1])
    wait_own(dv_out.at[:, pl.ds(0, HEAD_SIZE)], own.at[2])


def attend(seq, order, table, q_late, g_late, ks, vs, dk, dv, early):
    tokens = ks.shape[0]
    rows = tokens // seq
    span = tokens // order.shape[0]
    smem = pl.BlockSpec(memory_space=pltpu.SMEM)
    hbm = pl.BlockSpec(memory_space=pl.ANY)
    low = jnp.bfloat16
    thin = (tokens, HEAD_SIZE)
    tall = (tokens, BLOCK)
    return pl.pallas_call(
        functools.partial(attend_kernel, seq, span),
        out_shape=(
            jax.ShapeDtypeStruct((rows, seq * GROUP * HEAD_SIZE), low),
            jax.ShapeDtypeStruct((rows, seq * HEAD_SIZE), low),
            jax.ShapeDtypeStruct((rows, seq * HEAD_SIZE), low),
        ),
        in_specs=[smem] + [hbm] * 8,
        out_specs=(hbm,) * 3,
        scratch_shapes=[
            pltpu.SMEM((tokens // span,), jnp.int32),
            pltpu.VMEM(thin, low),
            pltpu.VMEM(thin, low),
            pltpu.VMEM(thin, jnp.float32),
            pltpu.VMEM(thin, jnp.float32),
            pltpu.VMEM(thin, jnp.float32),
            pltpu.VMEM((UNIT,) + thin, low),
            pltpu.VMEM((UNIT,) + thin, low),
            pltpu.VMEM((HEAD_SIZE, tokens), low),
            pltpu.VMEM((tokens // span, span, HEAD_SIZE), low),
            pltpu.VMEM((tokens // span, span, HEAD_SIZE), low),
            pltpu.VMEM(thin, jnp.float32),
            pltpu.VMEM(thin, jnp.float32),
            pltpu.VMEM((2, UNIT) + tall, jnp.float32),
            pltpu.VMEM((2, UNIT) + tall, jnp.float32),
            pltpu.VMEM((UNIT, tokens // span, span, HEAD_SIZE), low),
            pltpu.VMEM((tokens // span, span, HEAD_SIZE), low),
            pltpu.VMEM((LATE,) + thin, low),
            pltpu.VMEM(thin, low),
            pltpu.VMEM(thin, low),
            pltpu.SemaphoreType.DMA((3,)),
            pltpu.SemaphoreType.DMA((3,)),
            pltpu.SemaphoreType.DMA((3,)),
            pltpu.SemaphoreType.DMA((2,)),
            pltpu.SemaphoreType.DMA((5,)),
        ],
        compiler_params=pltpu.CompilerParams(
            collective_id=0, has_side_effects=True, vmem_limit_bytes=25 << 20
        ),
        name="attend",
    )(order, q_late, ks, vs, g_late, table, dk, dv, early)


def store_kernel(*refs):
    sources, targets, sem = refs[:3], refs[3:6], refs[6]
    copies = [
        pltpu.make_async_copy(source, target, sem.at[index])
        for index, (source, target) in enumerate(zip(sources, targets))
    ]
    for copy in copies:
        copy.start()
    for copy in copies:
        copy.wait()


def store(results):
    any_spec = pl.BlockSpec(memory_space=pl.ANY)
    return pl.pallas_call(
        store_kernel,
        out_shape=tuple(jax.ShapeDtypeStruct(a.shape, a.dtype) for a in results),
        in_specs=[any_spec] * 3,
        out_specs=(any_spec,) * 3,
        scratch_shapes=[pltpu.SemaphoreType.DMA((3,))],
        compiler_params=pltpu.CompilerParams(vmem_limit_bytes=2 << 20),
        name="store",
    )(*results)


def body(sections, seq, q, k, v, g, partner, order):
    table = jnp.asarray(rotary_table(q.shape[2] * seq))
    span = q.shape[2] * seq // order.shape[0]
    parts = [a.reshape(-1, span, a.shape[-1]) for a in (q, k, v, g)]
    branches = [functools.partial(gather, pair, seq) for pair in range(1, sections)]
    moved = lax.switch(partner[0] - 1, branches, order, *parts, table)
    results = attend(seq, order, table, *moved)
    return tuple(result[None, None] for result in store(results))


def solution(mesh):
    placed = P("section", None, "seq", None)
    return jax.shard_map(
        functools.partial(body, mesh.shape["section"], mesh.shape["seq"]),
        mesh=mesh,
        in_specs=(placed, placed, placed, placed, P(), P()),
        out_specs=(placed, placed, placed),
        check_vma=False,
    )
```
